256 devices in a mesh: ctx: 32 (over x, z_hi, y), exp: 8 (over z_lo, core).
Axes of the slice: x: 4, y: 4, z: 8 (z_hi: 2, z_lo: 4; z = z_hi * 4 + z_lo), core: 2. Of those that a mesh axis runs over, the one named last changes fastest.
Arguments:
- queries: bfloat16 [256, 32, 128], P(None, 'exp'), may hold values from -64 to 64
- keys: bfloat16 [32768, 8, 128], P('ctx', 'exp'), may hold values from -8 to 8
- values: bfloat16 [32768, 8, 128], P('ctx', 'exp'), may hold values from -32 to 32
- out_proj: bfloat16 [4096, 4096], P('exp', 'ctx'), may hold values from -0.09375 to 0.09375
- residual: bfloat16 [256, 4096], P('ctx'), may hold values from -6 to 6
- gain: float32 [4096], replicated, may hold values from 0.1 to 1.9
- routes: int32 [256, 2], P('ctx'), may hold values from 0 to 7, all different within a row; in each aligned block of 8 rows (0 to 7, 8 to 15, ...) at most 4 rows name the same one
- gates: float32 [256, 2], P('ctx'), may hold values from 0.25 to 1
- w_gate: bfloat16 [8, 4096, 14336], P('exp', None, 'ctx'), may hold values from -0.09375 to 0.09375
- w_up: bfloat16 [8, 4096, 14336], P('exp', None, 'ctx'), may hold values from -0.09375 to 0.09375
- w_down: bfloat16 [8, 14336, 4096], P('exp', 'ctx'), may hold values from -0.046875 to 0.046875
Outputs:
- mixed: bfloat16 [256, 4096], P('ctx', 'exp')
The draws below stay inside these ranges and needn't reach their ends.
Inputs may be any that keep to these rules, and one draw needn't show every extreme that they name: `routes`: within each aligned block of 8 rows no expert is named by more than 4 rows, some expert is named by exactly 4 rows in some block, and the 2 experts of a row differ.
All inputs are finite; a program needn't handle non-finite values.
Results may differ from the reference program's by a relative error of at most 0.017.
Values may be sent and summed in bfloat16 or wider, within the bound.
A program may use at most 128 MiB of HBM per device.

```python
import math
import jax
import jax.numpy as jnp
import numpy as np
from jax import lax

D = 4096
HEADS = 32
KVH = 8
HD = 128
TOP = 2
FFW = 14336
TOK_BLK = 8
CTX_DEV = 1024
TOKENS = 256
LEN = 32768
EXPERTS = 8
CAP = 4
FF_DEV = 448


def planted(key):
    base_key = jax.random.fold_in(key, 101)
    sign_key, first_key, second_key = jax.random.split(base_key, 3)
    signs = jnp.where(jax.random.bernoulli(sign_key, 0.5, (KVH, HD)), 1.0, -1.0).astype(jnp.float32)
    first_pos = jax.random.randint(first_key, (KVH,), 0, LEN // 2)
    second_pos = jax.random.randint(second_key, (KVH,), LEN // 2, LEN - TOKENS)
    return (signs, first_pos, second_pos)


def draw_keys(key, part):
    signs, first_pos, second_pos = planted(key)
    noise_key = jax.random.fold_in(key, 102)
    noise = jax.random.normal(noise_key, (LEN, KVH, HD), jnp.float32)
    positions = jnp.arange(LEN)[:, None, None]
    noise = jnp.where(positions == first_pos[None, :, None], signs[None], noise)
    noise = jnp.where(positions == second_pos[None, :, None], 0.988 * signs[None], noise)
    return jnp.clip(noise, -8.0, 8.0).astype(jnp.bfloat16)


def draw_queries(key, part):
    noise_key = jax.random.fold_in(key, 103)
    wide_key = jax.random.fold_in(key, 106)
    pick_key = jax.random.fold_in(key, 107)
    token_ids = jnp.arange(TOKENS)[:, None, None]
    picked = jax.random.bernoulli(pick_key, 0.125, (TOKENS, 1, 1)) & (token_ids % 16 != 3)
    base = 3.0 * jax.random.normal(noise_key, (TOKENS, HEADS, HD), jnp.float32)
    wide = 20.0 * jax.random.normal(wide_key, (TOKENS, HEADS, HD), jnp.float32)
    base = jnp.where(picked, wide, base)
    return jnp.clip(base, -64.0, 64.0).astype(jnp.bfloat16)


def draw_values(key, part):
    mean_key = jax.random.fold_in(key, 104)
    noise_key = jax.random.fold_in(key, 105)
    means = 6.0 * jax.random.normal(mean_key, (LEN // 512, KVH, HD), jnp.float32)
    noise = 2.0 * jax.random.normal(noise_key, (LEN, KVH, HD), jnp.float32)
    return jnp.clip(jnp.repeat(means, 512, axis=0) + noise, -32.0, 32.0).astype(jnp.bfloat16)


def shard_levels(stream_key, dims, cuts, least, largest):
    def one(position, blocks):
        steps = jax.random.uniform(jax.random.fold_in(jax.random.fold_in(stream_key, 6), position), (blocks,), jnp.float32, least / len(cuts), largest / len(cuts))
        return jnp.repeat(jnp.exp(steps), dims[position] // blocks).reshape((-1,) + (1,) * (len(dims) - position - 1))

    level = one(*cuts[0])
    for cut in cuts[1:]:
        level = level * one(*cut)
    return level


def deal_out(rng, own, number, rows, count, top, most, lean):
    sequence = jax.random.permutation(rng, count)
    packed, ordinary = portions_of(count, rows * top, most, lean, True), portions_of(count, rows * top, most, lean, False)
    places = jnp.arange(count)

    def named(tallies, offset_by):
        used = int((tallies > 0).sum())
        fixed = max(1, used // 4)
        passed = fixed + (places - fixed + offset_by * (used - fixed)) % max(1, count - fixed)
        return jnp.zeros((count,), jnp.int32).at[sequence[jnp.where(places < fixed, places, passed)]].set(jnp.asarray(tallies, jnp.int32))

    tallies = jnp.where(number % 4 == 0, named(packed, number // 4), named(ordinary, number - number // 4 - 1))
    mixed = jax.random.permutation(jax.random.fold_in(own, 3), count)
    source_of, taker = mixed[0:count // 2 * 2:2], mixed[1:count // 2 * 2:2]
    room = jnp.minimum(tallies[source_of] - 1, most - tallies[taker]) // 2
    room = jnp.where((source_of == sequence[0]) | (taker == sequence[0]) | (tallies[taker] == 0), 0, jnp.maximum(room, 0))
    passed = jax.random.randint(jax.random.fold_in(own, 4), (count // 2,), 0, 1 << 20) % (room + 1)
    tallies = tallies.at[source_of].add(-passed).at[taker].add(passed)
    items = jnp.searchsorted(jnp.cumsum(tallies), jnp.arange(rows * top), side="right").astype(jnp.int32)
    table = items.reshape(top, rows).T
    table = table[jax.random.permutation(jax.random.fold_in(own, 1), rows)]
    offset_by = jax.random.randint(jax.random.fold_in(own, 2), (rows, 1), 0, top)
    return jnp.take_along_axis(table, (jnp.arange(top)[None, :] + offset_by) % top, axis=1)


def portions_of(count, total, reach, skew, full):
    portions = [(1 << 20) // math.isqrt(grade ** skew) + 1 for grade in range(1, count + 1)]
    largest = reach if full else min(reach, max(-(-total // count), total * portions[0] // sum(portions)))
    least = 1 if total - largest >= count - 1 else 0
    holding, rest = [largest] + [least] * (count - 1), total - largest - least * (count - 1)
    while rest > 0:
        free = [i for i in range(1, count) if holding[i] < largest] or [i for i in range(1, count) if holding[i] < reach]
        whole, left = sum([portions[i] for i in free]), rest
        for i in free:
            extra = min(reach - holding[i], max(1, left * portions[i] // whole), rest)
            holding[i] = holding[i] + extra
            rest = rest - extra
    return np.array(holding)


def normal_values(rng, extent, deviation, limit, cuts=(), kind=jnp.bfloat16):
    array = deviation * jax.random.normal(rng, extent, jnp.float32)
    if cuts:
        array = array * shard_levels(rng, extent, cuts, -0.22, 0.18)
    return jnp.clip(array, -limit, limit).astype(kind)


def setup_inputs(seed: int = 0) -> dict:
    arg_keys = jax.random.split(jax.random.key(seed), 12)
    queries = draw_queries(jax.random.fold_in(arg_keys[11], 71), 0)
    keys = draw_keys(jax.random.fold_in(arg_keys[11], 71), 0)
    values = draw_values(jax.random.fold_in(arg_keys[11], 71), 0)
    out_proj = normal_values(arg_keys[3], (HEADS * HD, D), (HEADS * HD) ** -0.5, 0.09375, ((0, 8), (1, 32)))
    residual = normal_values(arg_keys[4], (TOKENS, D), 1.0, 6.0, ((0, 32),))
    gain = jnp.clip(1.0 + 0.18 * jax.random.normal(arg_keys[5], (D,), jnp.float32), 0.1, 1.9)
    routes_keys = jax.random.split(jax.random.fold_in(arg_keys[6], 1), TOKENS // TOK_BLK)
    routes_turns = jax.random.permutation(jax.random.fold_in(arg_keys[6], 3), TOKENS // TOK_BLK)
    routes = jax.vmap(lambda own, number: deal_out(jax.random.fold_in(arg_keys[6], 2), own, number, TOK_BLK, EXPERTS, TOP, CAP, 2))(routes_keys, routes_turns).reshape((TOKENS, TOP))
    gates = jnp.clip(0.25 + 0.75 * jax.random.uniform(arg_keys[7], (TOKENS, TOP), jnp.float32) ** shard_levels(arg_keys[7], (TOKENS, TOP), ((0, 32),), -0.2, 0.2), 0.25, 1.0)
    w_gate = normal_values(arg_keys[8], (EXPERTS, D, FFW), D ** -0.5, 0.09375, ((0, 8), (2, 32)))
    w_up = normal_values(arg_keys[9], (EXPERTS, D, FFW), D ** -0.5, 0.09375, ((0, 8), (2, 32)))
    w_down = normal_values(arg_keys[10], (EXPERTS, FFW, D), FFW ** -0.5, 0.046875, ((0, 8), (1, 32)))
    return {"queries": queries, "keys": keys, "values": values, "out_proj": out_proj, "residual": residual, "gain": gain, "routes": routes, "gates": gates, "w_gate": w_gate, "w_up": w_up, "w_down": w_down}


def pick_rows(block_rows, index_table):
    return block_rows[index_table]

def reference(queries, keys, values, out_proj, residual, gain, routes, gates, w_gate, w_up, w_down):
    groups = HEADS // KVH
    block_total = LEN // CTX_DEV
    score_scale = 1.0 / math.sqrt(HD)
    query_pos = LEN - TOKENS + jnp.arange(TOKENS, dtype=jnp.int32)

    def per_group(group_id):
        query_group = lax.dynamic_slice_in_dim(queries, group_id * groups, groups, 1).astype(jnp.float32)
        key_group = lax.dynamic_index_in_dim(keys, group_id, 1, keepdims=False)
        value_group = lax.dynamic_index_in_dim(values, group_id, 1, keepdims=False)

        def step(carry, block_id):
            run_max, run_sum, run_out = carry
            first = block_id * CTX_DEV
            key_block = lax.dynamic_slice_in_dim(key_group, first, CTX_DEV, 0).astype(jnp.float32)
            value_block = lax.dynamic_slice_in_dim(value_group, first, CTX_DEV, 0).astype(jnp.float32)
            scores = jnp.einsum('trd,sd->trs', query_group, key_block) * score_scale
            key_pos = first + jnp.arange(CTX_DEV, dtype=jnp.int32)
            visible = key_pos[None, None, :] <= query_pos[:, None, None]
            scores = jnp.where(visible, scores, jnp.float32(-1e+30))
            block_max = lax.optimization_barrier(jnp.max(scores, axis=-1))
            expw = jnp.where(visible, jnp.exp(scores - block_max[..., None]), jnp.float32(0.0))
            block_sum = lax.optimization_barrier(jnp.sum(expw, axis=-1))
            probs = expw.astype(jnp.bfloat16)
            block_out = jnp.einsum('trs,sd->trd', probs.astype(jnp.float32), value_block)
            new_max = jnp.maximum(run_max, block_max)
            old_scale = jnp.exp(run_max - new_max)
            new_scale = jnp.exp(block_max - new_max)
            run_sum = run_sum * old_scale + block_sum * new_scale
            run_out = run_out * old_scale[..., None] + block_out * new_scale[..., None]
            return ((new_max, run_sum, run_out), None)
        start_state = (jnp.full((TOKENS, groups), -1e+30, jnp.float32), jnp.zeros((TOKENS, groups), jnp.float32), jnp.zeros((TOKENS, groups, HD), jnp.float32))
        final_state, unused = lax.scan(step, start_state, jnp.arange(block_total, dtype=jnp.int32))
        return final_state[2] / final_state[1][..., None]
    per_head = lax.map(per_group, jnp.arange(KVH, dtype=jnp.int32))
    attended = per_head.transpose(1, 0, 2, 3).reshape(TOKENS, HEADS * HD).astype(jnp.bfloat16)
    stream = residual.astype(jnp.float32) + jnp.dot(attended, out_proj, preferred_element_type=jnp.float32)
    normed = (stream * lax.rsqrt(lax.optimization_barrier(jnp.mean(stream * stream, axis=-1, keepdims=True)) + 1e-05) * gain).astype(jnp.bfloat16)
    block_count = TOKENS // TOK_BLK
    flat_ids = routes.reshape(block_count, TOK_BLK * TOP)
    onehot = (flat_ids[:, :, None] == jnp.arange(EXPERTS, dtype=jnp.int32)[None, None, :]).astype(jnp.int32)
    before = jnp.cumsum(onehot, axis=1, dtype=jnp.int32) - onehot
    slot_of = lax.optimization_barrier(jnp.sum(before * onehot, axis=-1, dtype=jnp.int32))
    token_of = jnp.arange(TOK_BLK * TOP, dtype=jnp.int32) // TOP
    block_ids = jnp.arange(block_count, dtype=jnp.int32)[:, None]
    table = jnp.full((block_count, EXPERTS, CAP), TOK_BLK, jnp.int32)
    table = table.at[block_ids, flat_ids, slot_of].set(jnp.broadcast_to(token_of[None, :], flat_ids.shape))
    padded = jnp.concatenate([normed.reshape(block_count, TOK_BLK, D), jnp.zeros((block_count, 1, D), jnp.bfloat16)], axis=1)
    buffer = jax.vmap(pick_rows)(padded, table)
    unit_groups = FFW // FF_DEV

    def run_expert(expert_id):
        rows = lax.dynamic_index_in_dim(buffer, expert_id, 1, keepdims=False).reshape(block_count * CAP, D)
        gate_val = jnp.dot(rows, w_gate[expert_id], preferred_element_type=jnp.float32)
        up_val = jnp.dot(rows, w_up[expert_id], preferred_element_type=jnp.float32)
        act = (jax.nn.silu(gate_val) * up_val).astype(jnp.bfloat16)
        down_mat = w_down[expert_id]

        def add_group(total, group_id):
            act_cols = lax.dynamic_slice_in_dim(act, group_id * FF_DEV, FF_DEV, 1)
            down_rows = lax.dynamic_slice_in_dim(down_mat, group_id * FF_DEV, FF_DEV, 0)
            term = jnp.dot(act_cols, down_rows, preferred_element_type=jnp.float32).astype(jnp.bfloat16)
            term = lax.optimization_barrier(term)
            return (total + term.astype(jnp.float32), None)
        start_total = jnp.zeros((block_count * CAP, D), jnp.float32)
        summed, unused = lax.scan(add_group, start_total, jnp.arange(unit_groups, dtype=jnp.int32))
        return summed.reshape(block_count, CAP, D)
    expert_out = lax.map(run_expert, jnp.arange(EXPERTS, dtype=jnp.int32))
    picked = expert_out[flat_ids, block_ids, slot_of].reshape(TOKENS, TOP, D)
    mixture = lax.optimization_barrier(jnp.sum(gates[:, :, None] * picked, axis=1))
    return (stream + mixture).astype(jnp.bfloat16)
```

```python
import functools
import math

import jax
import jax.numpy as jnp
from jax import lax
from jax.experimental import pallas as pl
from jax.experimental.pallas import tpu as pltpu
from jax.sharding import PartitionSpec as P

F32 = jnp.float32
BF16 = jnp.bfloat16
PLANE = (4, 4)
CAP = 4
VMEM_LIMIT = 56 * 1024 * 1024


def iota(shape, dim):
    return lax.broadcasted_iota(jnp.int32, shape, dim)


def div(a, b):
    return lax.div(a, jnp.int32(b))


def rem(a, b):
    return lax.rem(a, jnp.int32(b))


def dot(a, b):
    return lax.dot_general(a, b, (((1,), (0,)), ((), ())), preferred_element_type=F32)


def dot_nt(a, b):
    return lax.dot_general(a, b, (((1,), (1,)), ((), ())), preferred_element_type=F32)


def wait_bytes(ref, sem):
    pltpu.make_async_copy(ref, ref, sem).wait()


def kernel(
    geom,
    q_ref, k_ref, v_ref, wo_ref, res_ref, gain_ref, routes_ref, gates_ref, wg_hbm, wu_hbm, wd_hbm,
    out_ref,
    abuf, arecv, wt_s, att_all, w_all, rs_send, rs_recv, res_recv, g_own, g_recv, gg_all, f_sel,
    z_send, xall, sq_acc, accg, accu, sown, e_send, e_recv, f_send, f_recv, wg_s, wu_s, wd_s,
    wsem, ssem, rsem, early, d_recv,
):
    X, Y, E, chunk_cols = geom
    PL, CTX = X * Y, 2 * X * Y
    PB = PL // E
    D = CTX * 128
    S = 2 * PL * CAP
    NCH, CE = D // chunk_cols, D // E
    tokens = CTX * 8
    key_rows = k_ref.shape[0]

    c = lax.axis_index("ctx")
    e = lax.axis_index("exp")
    x = div(c, 2 * Y)
    h = rem(div(c, Y), 2)
    y = rem(c, Y)
    p = x * Y + y
    hz = h * E + e

    def at_plane(pp):
        return div(pp, Y) * (2 * Y) + h * Y + rem(pp, Y)

    def at_z(hh):
        return x * (2 * Y) + hh * Y + y

    def send(src, dst, ssem_, rsem_, ctx, exp):
        pltpu.make_async_remote_copy(
            src_ref=src, dst_ref=dst, send_sem=ssem_, recv_sem=rsem_,
            device_id={"ctx": ctx, "exp": exp}, device_id_type=pl.DeviceIdType.MESH,
        ).start()

    barrier = pltpu.get_barrier_semaphore()

    @pl.loop(1, CTX)
    def _(i):
        pl.semaphore_signal(
            barrier, inc=1, device_id={"ctx": rem(c + i, CTX), "exp": e},
            device_id_type=pl.DeviceIdType.MESH,
        )

    @pl.loop(1, E)
    def _(i):
        for hh in range(2):
            pl.semaphore_signal(
                barrier, inc=1, device_id={"ctx": at_z(hh), "exp": rem(e + i, E)},
                device_id_type=pl.DeviceIdType.MESH,
            )

    weights = [
        pltpu.make_async_copy(a, b, wsem.at[i])
        for i, (a, b) in enumerate(((wg_hbm, wg_s), (wu_hbm, wu_s), (wd_hbm, wd_s)))
    ]
    for w in weights:
        w.start()

    lane8 = iota((8, 128), 1)
    row8 = iota((8, 128), 0)
    route = [routes_ref[:, k : k + 1] for k in range(2)]
    gate = [gates_ref[:, k : k + 1] for k in range(2)]
    hit = jnp.where((lane8 == route[0]) | (lane8 == route[1]), 1.0, 0.0)
    before = jnp.zeros((8, 128), F32)
    for t in range(7):
        before = before + jnp.where(row8 > t, hit[t : t + 1, :], 0.0)
    slot = [
        jnp.sum(jnp.where(lane8 == route[k], before, 0.0), axis=1, keepdims=True).astype(jnp.int32)
        for k in range(2)
    ]
    place = [route[k] * CAP + slot[k] for k in range(2)]
    g_own[...] = jnp.where((lane8 == place[0]) | (lane8 == place[1]), 1.0, 0.0)
    own_gates = jnp.where(lane8 == place[0], gate[0], 0.0) + jnp.where(
        lane8 == place[1], gate[1], 0.0
    )
    gg_all[pl.ds(h, 1)] = own_gates[None]
    row_s = iota((8, S), 1)
    f_sel[...] = jnp.where(
        (div(row_s, CAP) == h * PL + p) & (route[0] == e) & (slot[0] == rem(row_s, CAP)), 1.0, 0.0
    ).astype(BF16)
    w_all[pl.ds(h, 1)] = wo_ref[...][None]

    scale = 1.0 / math.sqrt(128)
    tail = key_rows - min(tokens, key_rows)

    def attend(j):
        q = q_ref[pl.ds(pl.multiple_of(j * 128, 128), 128), :]
        s = dot_nt(q, k_ref[...]) * scale
        row = j * 128 + iota((128, key_rows - tail), 0)
        token = div(row, 32) * 8 + rem(row, 8)
        limit = (CTX * key_rows - tokens) - c * key_rows + token
        masked = jnp.where(
            tail + iota((128, key_rows - tail), 1) <= limit, s[:, tail:], jnp.float32(-1e30)
        )
        s = jnp.concatenate([s[:, :tail], masked], axis=1) if tail else masked
        m = jnp.max(s, axis=1, keepdims=True)
        w = jnp.exp(s - m)
        total = jnp.sum(w, axis=1, keepdims=True)
        o = (dot(w.astype(BF16), v_ref[...]) / total).astype(BF16)
        lse = m + jnp.log(total)
        flat = jnp.sum(
            jnp.where(iota((128, 128), 0) == iota((128, 128), 1), lse, 0.0), axis=0, keepdims=True
        )
        hi = flat.astype(BF16).astype(F32)
        mid = (flat - hi).astype(BF16).astype(F32)
        lo = flat - hi - mid
        lines = jnp.where(
            row8 == 0, hi, jnp.where(row8 == 1, mid, jnp.where(row8 == 2, lo, 0.0))
        ).astype(BF16)
        for r in range(4):
            abuf[j * 4 + r, 0:32, :] = o[r * 32 : (r + 1) * 32, :]
            abuf[j * 4 + r, 32:40, :] = lines

    def send_chunk(j):
        for r in range(4):
            dest = j * 4 + r

            @pl.when(dest != c)
            def _():
                send(abuf.at[dest], arecv.at[c], ssem.at[0], rsem.at[0], dest, e)

    n_chunks = CTX // 4
    first = rem(div(c, 4) + 1, n_chunks)
    attend(first)
    pl.semaphore_wait(barrier, CTX - 1 + 2 * (E - 1))

    send(wo_ref, w_all.at[h], ssem.at[7], early.at[0], at_z(1 - h), e)
    send(gg_all.at[h], gg_all.at[h], ssem.at[8], early.at[1], at_z(1 - h), e)
    spread = div(p, PB) == e
    mine = rem(p, PB)

    @pl.when(spread)
    def _():
        @pl.loop(1, PL)
        def _(i):
            pp = rem(p + i, PL)
            there = at_plane(pp)
            low = div(pp, Y) * (2 * Y) + rem(pp, Y)
            for half in range(2):
                cols = pl.ds(pl.multiple_of((low + half * Y) * 128, 128), 128)
                send(res_ref.at[:, cols], res_recv.at[mine, half], ssem.at[9], early.at[2 + mine], there, e)
            send(g_own, g_recv.at[mine], ssem.at[10], early.at[2 + PB + mine], there, e)

        low = x * (2 * Y) + y
        for half in range(2):
            cols = pl.ds(pl.multiple_of((low + half * Y) * 128, 128), 128)
            res_recv[pl.ds(mine, 1), half] = res_ref[:, cols][None]
        g_recv[pl.ds(mine, 1)] = g_own[...][None]

    send_chunk(first)

    @pl.loop(1, n_chunks)
    def _(i):
        j = rem(first + i, n_chunks)
        attend(j)
        send_chunk(j)

    arecv[pl.ds(c, 1)] = abuf[pl.ds(c, 1)]
    wait_bytes(arecv.at[pl.ds(0, CTX - 1)], rsem.at[0])
    levels = jnp.zeros((CTX, 128), F32)
    for i in range(CTX):
        line = jnp.sum(arecv[i, 32:40, :].astype(F32), axis=0, keepdims=True)
        levels = jnp.where(iota((CTX, 128), 0) == i, line, levels)
    weight = jnp.exp(levels - jnp.max(levels, axis=0, keepdims=True))
    weight = weight / jnp.sum(weight, axis=0, keepdims=True)
    weight = jnp.concatenate([weight, jnp.zeros((128 - CTX, 128), F32)], axis=0)
    wt_s[...] = weight.T
    columns = wt_s[pl.ds(pl.multiple_of(rem(c, 4) * 32, 32), 32), :]
    attended = jnp.zeros((32, 128), F32)
    for i in range(CTX):
        attended = attended + arecv[i, 0:32, :].astype(F32) * columns[:, i : i + 1]
    att_all[pl.ds(p, 1)] = attended.astype(BF16)[None]

    @pl.loop(1, PL)
    def _(i):
        send(att_all.at[p], att_all.at[p], ssem.at[1], rsem.at[1], at_plane(rem(p + i, PL)), e)

    wait_bytes(wo_ref, early.at[0])
    projections = [
        jnp.concatenate([w_all[hh, r * 128 : (r + 1) * 128, :] for hh in range(2)], axis=1)
        for r in range(4)
    ]
    wait_bytes(att_all.at[pl.ds(0, PL - 1)], rsem.at[1])
    rows = att_all[...].reshape(PL * 32, 128)
    partial = jnp.zeros((PL, 8, 256), F32)
    for r in range(4):
        partial = partial + dot(rows, projections[r]).reshape(PL, 4, 8, 256)[:, r]
    rs_send[...] = partial.reshape(E, PB * 8, 256).astype(BF16)
    rs_recv[pl.ds(e, 1)] = rs_send[pl.ds(e, 1)]

    @pl.loop(1, E)
    def _(i):
        ee = rem(e + i, E)
        send(rs_send.at[ee], rs_recv.at[e], ssem.at[2], rsem.at[2], c, ee)

    for i in range(PB):

        @pl.when(p != e * PB + i)
        def _():
            wait_bytes(res_recv.at[i], early.at[2 + i])
            wait_bytes(g_recv.at[i], early.at[2 + PB + i])

    pick_rows = E * PB * CAP
    table = g_recv[...].reshape(PB * 8, 128).astype(BF16)
    pick = iota((pick_rows, 128), 0)
    chooser = jnp.where(
        iota((pick_rows, 128), 1) == div(pick, PB * CAP) * CAP + rem(pick, CAP), 1.0, 0.0
    ).astype(BF16)
    picks = dot_nt(chooser, table)
    pick = iota((pick_rows, PB * 8), 0)
    picks = jnp.where(
        rem(div(pick, CAP), PB) == div(iota((pick_rows, PB * 8), 1), 8), picks, 0.0
    ).astype(BF16)
    residual = jnp.concatenate(
        [
            jnp.concatenate([res_recv[i, half].astype(F32) for half in range(2)], axis=1)
            for i in range(PB)
        ],
        axis=0,
    )

    wait_bytes(rs_recv.at[pl.ds(0, E - 1)], rsem.at[2])
    stream = residual
    for i in range(E):
        stream = stream + rs_recv[i].astype(F32)
    z_send[...] = dot(picks, stream.astype(BF16)).reshape(E, PB * CAP, 256).astype(BF16)
    xall[pl.ds(p, 1), pl.ds(hz, 1)] = z_send[pl.ds(e, 1)][None]

    @pl.loop(1, 2 * E)
    def _(i):
        zz = rem(hz + i, 2 * E)
        ee = rem(zz, E)
        send(z_send.at[ee], xall.at[p, hz], ssem.at[3], rsem.at[3], at_z(div(zz, E)), ee)

    sq_acc[...] = jnp.zeros_like(sq_acc)
    accg[...] = jnp.zeros_like(accg)
    accu[...] = jnp.zeros_like(accu)
    weights[0].wait()
    weights[1].wait()
    wait_bytes(xall.at[p, pl.ds(0, 2 * E - 1)], rsem.at[3])

    @pl.loop(1, PL)
    def _(i):
        xx = rem(x + div(i, Y), X)
        yy = rem(y + rem(i, Y), Y)
        send(xall.at[p], xall.at[p], ssem.at[4], d_recv.at[i], xx * (2 * Y) + h * Y + yy, e)

    @pl.loop(0, PL)
    def _(i):
        xx = rem(x + X - div(i, Y), X)
        yy = rem(y + Y - rem(i, Y), Y)
        src = xx * Y + yy

        @pl.when(i > 0)
        def _():
            wait_bytes(xall.at[src], d_recv.at[i])

        part = xall[src].astype(F32).reshape(S, 256)
        sq_acc[...] += part[:, :128] * part[:, :128] + part[:, 128:] * part[:, 128:]
        low = pl.multiple_of((xx * (2 * Y) + yy) * 128, 128)
        high = pl.multiple_of((xx * (2 * Y) + Y + yy) * 128, 128)
        scaled = (part * gain_ref[src]).astype(BF16)
        for acc, w in ((accg, wg_s), (accu, wu_s)):
            block = jnp.concatenate([w[:, pl.ds(low, 128)], w[:, pl.ds(high, 128)]], axis=1)
            acc[...] += dot_nt(scaled, block)
        own = dot(f_sel[...], part.astype(BF16))
        sown[:, pl.ds(low, 128)] = own[:, :128]
        sown[:, pl.ds(high, 128)] = own[:, 128:]

    norm = lax.rsqrt(jnp.sum(sq_acc[...], axis=1, keepdims=True) / D + 1e-05)
    gate_val = accg[...] * norm
    act = ((gate_val / (1.0 + jnp.exp(-gate_val))) * (accu[...] * norm)).astype(BF16)
    new = iota((S, S), 0)
    order = rem(div(new, CAP), 2) * (PL * CAP) + div(new, 2 * CAP) * CAP + rem(new, CAP)
    act = dot(jnp.where(iota((S, S), 1) == order, 1.0, 0.0).astype(BF16), act).astype(BF16)

    weights[2].wait()
    for n in range(NCH):
        down = dot(act, wd_s[:, n * chunk_cols : (n + 1) * chunk_cols])
        e_send[n] = down.reshape(PL, 2 * CAP, chunk_cols).astype(BF16)
        e_recv[n, pl.ds(p, 1)] = e_send[n, pl.ds(p, 1)]

        @pl.loop(1, PL)
        def _(i):
            xx = rem(x + div(i, Y), X)
            yy = rem(y + rem(i, Y), Y)
            send(
                e_send.at[n, xx * Y + yy], e_recv.at[n, p], ssem.at[5], rsem.at[5 + n],
                xx * (2 * Y) + h * Y + yy, e,
            )

    wait_bytes(gg_all.at[h], early.at[1])
    weigh = [
        [
            jnp.sum(jnp.where(lane8 == e * CAP + s, gg_all[hh], 0.0), axis=1, keepdims=True)
            for s in range(CAP)
        ]
        for hh in range(2)
    ]
    for n in range(NCH):
        wait_bytes(e_recv.at[n, pl.ds(0, PL - 1)], rsem.at[5 + n])
        total = jnp.sum(e_recv[n].astype(F32), axis=0)
        for f in range(chunk_cols // CE):
            ee = n * (chunk_cols // CE) + f
            stream_own = sown[:, ee * CE : (ee + 1) * CE]
            for hh in range(2):
                term = jnp.where(h == hh, stream_own, 0.0)
                for s in range(CAP):
                    line = hh * CAP + s
                    term = term + weigh[hh][s] * total[line : line + 1, f * CE : (f + 1) * CE]
                f_send[hh * E + ee] = term.astype(BF16)
                away = (h != hh) | (e != ee)

                @pl.when(away)
                def _():
                    send(f_send.at[hh * E + ee], f_recv.at[hz], ssem.at[6], rsem.at[4], at_z(hh), ee)

    f_recv[pl.ds(hz, 1)] = f_send[pl.ds(hz, 1)]
    wait_bytes(f_recv.at[pl.ds(0, 2 * E - 1)], rsem.at[4])
    out_ref[...] = jnp.sum(f_recv[...].astype(F32), axis=0).astype(BF16)

    wait_bytes(abuf.at[pl.ds(0, CTX - 1)], ssem.at[0])
    wait_bytes(att_all.at[pl.ds(0, PL - 1)], ssem.at[1])
    wait_bytes(rs_send.at[pl.ds(0, E - 1)], ssem.at[2])
    wait_bytes(xall.at[0, pl.ds(0, 2 * E - 1)], ssem.at[3])
    wait_bytes(xall.at[pl.ds(0, PL - 1)], ssem.at[4])
    wait_bytes(e_send.at[:, pl.ds(0, PL - 1)], ssem.at[5])
    wait_bytes(f_send.at[pl.ds(0, 2 * E - 1)], ssem.at[6])
    wait_bytes(wo_ref, ssem.at[7])
    wait_bytes(gg_all.at[h], ssem.at[8])

    @pl.when(spread)
    def _():
        wait_bytes(f_recv.at[pl.ds(0, PL - 1), :, pl.ds(0, 256)], ssem.at[9])
        wait_bytes(f_recv.at[pl.ds(0, PL - 1), :, pl.ds(0, 256)], ssem.at[10])


def local(queries, keys, values, out_proj, residual, gain, routes, gates, w_gate, w_up, w_down):
    X, Y = PLANE
    CTX, PL, E = 2 * X * Y, X * Y, lax.axis_size("exp")
    PB, D, FF = PL // E, gain.shape[0], w_gate.shape[2]
    S, CE = 2 * PL * CAP, D // E
    chunk_cols = 1024
    NCH = D // chunk_cols
    q = queries.reshape(CTX, 8, 4, 128).transpose(0, 2, 1, 3).reshape(CTX * 32, 128)
    gains = gain.reshape(X, 2, Y, 128).transpose(0, 2, 1, 3).reshape(PL, 1, 256)
    vmem = pl.BlockSpec(memory_space=pltpu.VMEM)
    return pl.pallas_call(
        functools.partial(kernel, (X, Y, E, chunk_cols)),
        out_shape=jax.ShapeDtypeStruct((8, CE), BF16),
        in_specs=[vmem] * 8 + [pl.BlockSpec(memory_space=pl.ANY)] * 3,
        out_specs=vmem,
        scratch_shapes=[
            pltpu.VMEM((CTX, 40, 128), BF16),
            pltpu.VMEM((CTX, 40, 128), BF16),
            pltpu.VMEM((128, 128), F32),
            pltpu.VMEM((PL, 32, 128), BF16),
            pltpu.VMEM((2, 512, 128), BF16),
            pltpu.VMEM((E, PB * 8, 256), BF16),
            pltpu.VMEM((E, PB * 8, 256), BF16),
            pltpu.VMEM((PB, 2, 8, 128), BF16),
            pltpu.VMEM((8, 128), F32),
            pltpu.VMEM((PB, 8, 128), F32),
            pltpu.VMEM((2, 8, 128), F32),
            pltpu.VMEM((8, S), BF16),
            pltpu.VMEM((E, PB * CAP, 256), BF16),
            pltpu.VMEM((PL, 2 * E, PB * CAP, 256), BF16),
            pltpu.VMEM((S, 128), F32),
            pltpu.VMEM((S, FF), F32),
            pltpu.VMEM((S, FF), F32),
            pltpu.VMEM((8, D), F32),
            pltpu.VMEM((NCH, PL, 2 * CAP, chunk_cols), BF16),
            pltpu.VMEM((NCH, PL, 2 * CAP, chunk_cols), BF16),
            pltpu.VMEM((2 * E, 8, CE), BF16),
            pltpu.VMEM((2 * E, 8, CE), BF16),
            pltpu.VMEM((FF, D), BF16),
            pltpu.VMEM((FF, D), BF16),
            pltpu.VMEM((FF, D), BF16),
            pltpu.SemaphoreType.DMA((3,)),
            pltpu.SemaphoreType.DMA((11,)),
            pltpu.SemaphoreType.DMA((5 + NCH,)),
            pltpu.SemaphoreType.DMA((2 + 2 * PB,)),
            pltpu.SemaphoreType.DMA((PL,)),
        ],
        compiler_params=pltpu.CompilerParams(
            collective_id=0, has_side_effects=True, vmem_limit_bytes=VMEM_LIMIT
        ),
    )(
        q,
        keys.reshape(keys.shape[0], 128),
        values.reshape(values.shape[0], 128),
        out_proj,
        residual,
        gains,
        routes,
        gates,
        jnp.swapaxes(w_gate, 1, 2).reshape(FF, D),
        jnp.swapaxes(w_up, 1, 2).reshape(FF, D),
        w_down.reshape(FF, D),
    )


def solution(mesh):
    return jax.shard_map(
        local,
        mesh=mesh,
        in_specs=(
            P(None, "exp", None),
            P("ctx", "exp", None),
            P("ctx", "exp", None),
            P("exp", "ctx"),
            P("ctx", None),
            P(),
            P("ctx", None),
            P("ctx", None),
            P("exp", None, "ctx"),
            P("exp", None, "ctx"),
            P("exp", "ctx", None),
        ),
        out_specs=P("ctx", "exp"),
        check_vma=False,
    )
```

```python
import functools
import math

import jax
import jax.numpy as jnp
from jax import lax
from jax.experimental import pallas as pl
from jax.experimental.pallas import tpu as pltpu
from jax.sharding import PartitionSpec as P

F32 = jnp.float32
BF16 = jnp.bfloat16
PLANE = (4, 4)
CAP = 4
VMEM_LIMIT = 56 * 1024 * 1024


def iota(shape, dim):
    return lax.broadcasted_iota(jnp.int32, shape, dim)


def div(a, b):
    return lax.div(a, jnp.int32(b))


def rem(a, b):
    return lax.rem(a, jnp.int32(b))


def dot(a, b):
    return lax.dot_general(a, b, (((1,), (0,)), ((), ())), preferred_element_type=F32)


def dot_nt(a, b):
    return lax.dot_general(a, b, (((1,), (1,)), ((), ())), preferred_element_type=F32)


def near_first(n):
    return sorted(range(1, n), key=lambda i: min(i, n - i))


def wait_bytes(ref, sem):
    pltpu.make_async_copy(ref, ref, sem).wait()


def kernel(
    geom,
    q_ref, k_ref, v_ref, wo_ref, res_ref, gain_ref, routes_ref, gates_ref, wg_hbm, wu_hbm, wd_hbm,
    out_ref,
    abuf, arecv, wt_s, att_all, w_all, rs_send, rs_recv, res_recv, g_own, g_recv, gg_all, f_sel,
    z_send, xall, sq_acc, accg, accu, sown, e_send, e_recv, t_send, t_recv, f_send, f_recv,
    wg_s, wu_s, wd_s,
    wsem, ssem, rsem, early, d_recv, e_sem, t_sem,
):
    X, Y, E, chunk_cols = geom
    PL, CTX = X * Y, 2 * X * Y
    PB = PL // E
    D = CTX * 128
    S = 2 * PL * CAP
    NCH, CE = D // chunk_cols, D // E
    tokens = CTX * 8
    key_rows = k_ref.shape[0]

    c = lax.axis_index("ctx")
    e = lax.axis_index("exp")
    x = div(c, 2 * Y)
    h = rem(div(c, Y), 2)
    y = rem(c, Y)
    p = x * Y + y
    hz = h * E + e

    def at_plane(pp):
        return div(pp, Y) * (2 * Y) + h * Y + rem(pp, Y)

    def at_z(hh):
        return x * (2 * Y) + hh * Y + y

    def send(src, dst, ssem_, rsem_, ctx, exp):
        pltpu.make_async_remote_copy(
            src_ref=src, dst_ref=dst, send_sem=ssem_, recv_sem=rsem_,
            device_id={"ctx": ctx, "exp": exp}, device_id_type=pl.DeviceIdType.MESH,
        ).start()

    barrier = pltpu.get_barrier_semaphore()

    @pl.loop(1, CTX)
    def _(i):
        pl.semaphore_signal(
            barrier, inc=1, device_id={"ctx": rem(c + i, CTX), "exp": e},
            device_id_type=pl.DeviceIdType.MESH,
        )

    @pl.loop(1, E)
    def _(i):
        for hh in range(2):
            pl.semaphore_signal(
                barrier, inc=1, device_id={"ctx": at_z(hh), "exp": rem(e + i, E)},
                device_id_type=pl.DeviceIdType.MESH,
            )

    weights = [
        pltpu.make_async_copy(a, b, wsem.at[i])
        for i, (a, b) in enumerate(((wg_hbm, wg_s), (wu_hbm, wu_s), (wd_hbm, wd_s)))
    ]
    for w in weights:
        w.start()

    lane8 = iota((8, 128), 1)
    row8 = iota((8, 128), 0)
    diagonal = iota((8, 8), 0) == iota((8, 8), 1)
    route = [
        jnp.sum(
            jnp.where(diagonal, routes_ref[k : k + 1, :].astype(F32), 0.0), axis=1, keepdims=True
        ).astype(jnp.int32)
        for k in range(2)
    ]
    gate = [
        jnp.sum(jnp.where(diagonal, gates_ref[k : k + 1, :], 0.0), axis=1, keepdims=True)
        for k in range(2)
    ]
    hit = jnp.where((lane8 == route[0]) | (lane8 == route[1]), 1.0, 0.0)
    before = jnp.zeros((8, 128), F32)
    for t in range(7):
        before = before + jnp.where(row8 > t, hit[t : t + 1, :], 0.0)
    slot = [
        jnp.sum(jnp.where(lane8 == route[k], before, 0.0), axis=1, keepdims=True).astype(jnp.int32)
        for k in range(2)
    ]
    place = [route[k] * CAP + slot[k] for k in range(2)]
    g_own[...] = jnp.where((lane8 == place[0]) | (lane8 == place[1]), 1.0, 0.0)
    own_gates = jnp.where(lane8 == place[0], gate[0], 0.0) + jnp.where(
        lane8 == place[1], gate[1], 0.0
    )
    gg_all[pl.ds(h, 1)] = own_gates[None]
    row_s = iota((8, S), 1)
    f_sel[...] = jnp.where(
        (div(row_s, CAP) == h * PL + p) & (route[0] == e) & (slot[0] == rem(row_s, CAP)), 1.0, 0.0
    ).astype(BF16)
    w_all[pl.ds(h, 1)] = wo_ref[...][None]

    scale = 1.0 / math.sqrt(128)
    tail = key_rows - min(tokens, key_rows)

    def attend(j):
        q = q_ref[pl.ds(pl.multiple_of(j * 128, 128), 128), :]
        s = dot_nt(q, k_ref[...]) * scale
        row = j * 128 + iota((128, key_rows - tail), 0)
        token = div(row, 4)
        limit = (CTX * key_rows - tokens) - c * key_rows + token
        masked = jnp.where(
            tail + iota((128, key_rows - tail), 1) <= limit, s[:, tail:], jnp.float32(-1e30)
        )
        s = jnp.concatenate([s[:, :tail], masked], axis=1) if tail else masked
        m = jnp.max(s, axis=1, keepdims=True)
        w = jnp.exp(s - m)
        total = jnp.sum(w, axis=1, keepdims=True)
        o = (dot(w.astype(BF16), v_ref[...]) / total).astype(BF16)
        lse = m + jnp.log(total)
        flat = jnp.sum(
            jnp.where(iota((128, 128), 0) == iota((128, 128), 1), lse, 0.0), axis=0, keepdims=True
        )
        hi = flat.astype(BF16).astype(F32)
        mid = (flat - hi).astype(BF16).astype(F32)
        lo = flat - hi - mid
        lines = jnp.where(
            row8 == 0, hi, jnp.where(row8 == 1, mid, jnp.where(row8 == 2, lo, 0.0))
        ).astype(BF16)
        for r in range(4):
            abuf[j * 4 + r, 0:32, :] = o[r * 32 : (r + 1) * 32, :]
            abuf[j * 4 + r, 32:40, :] = lines

    def send_chunk(j):
        for r in range(4):
            dest = j * 4 + r

            @pl.when(dest != c)
            def _():
                send(abuf.at[dest], arecv.at[c], ssem.at[0], rsem.at[0], dest, e)

    n_chunks = CTX // 4
    first = rem(div(c, 4) + 1, n_chunks)
    attend(first)
    pl.semaphore_wait(barrier, CTX - 1 + 2 * (E - 1))

    send(gg_all.at[h], gg_all.at[h], ssem.at[8], early.at[1], at_z(1 - h), e)
    spread = div(p, PB) == e
    mine = rem(p, PB)

    @pl.when(spread)
    def _():
        @pl.loop(1, PL)
        def _(i):
            pp = rem(p + i, PL)
            there = at_plane(pp)
            low = div(pp, Y) * (2 * Y) + rem(pp, Y)
            for half in range(2):
                cols = pl.ds(pl.multiple_of((low + half * Y) * 128, 128), 128)
                send(res_ref.at[:, cols], res_recv.at[mine, half], ssem.at[9], early.at[2 + mine], there, e)
            send(g_own, g_recv.at[mine], ssem.at[10], early.at[2 + PB + mine], there, e)

        low = x * (2 * Y) + y
        for half in range(2):
            cols = pl.ds(pl.multiple_of((low + half * Y) * 128, 128), 128)
            res_recv[pl.ds(mine, 1), half] = res_ref[:, cols][None]
        g_recv[pl.ds(mine, 1)] = g_own[...][None]

    send_chunk(first)

    @pl.loop(1, n_chunks)
    def _(i):
        j = rem(first + i, n_chunks)
        attend(j)
        send_chunk(j)

    send(wo_ref, w_all.at[h], ssem.at[7], early.at[0], at_z(1 - h), e)

    arecv[pl.ds(c, 1)] = abuf[pl.ds(c, 1)]
    wait_bytes(arecv.at[pl.ds(0, CTX - 1)], rsem.at[0])
    levels = jnp.zeros((CTX, 128), F32)
    for i in range(CTX):
        line = jnp.sum(arecv[i, 32:40, :].astype(F32), axis=0, keepdims=True)
        levels = jnp.where(iota((CTX, 128), 0) == i, line, levels)
    weight = jnp.exp(levels - jnp.max(levels, axis=0, keepdims=True))
    weight = weight / jnp.sum(weight, axis=0, keepdims=True)
    weight = jnp.concatenate([weight, jnp.zeros((128 - CTX, 128), F32)], axis=0)
    wt_s[...] = weight.T
    columns = wt_s[pl.ds(pl.multiple_of(rem(c, 4) * 32, 32), 32), :]
    attended = jnp.zeros((32, 128), F32)
    for i in range(CTX):
        attended = attended + arecv[i, 0:32, :].astype(F32) * columns[:, i : i + 1]
    new = iota((32, 32), 0)
    order = rem(new, 8) * 4 + div(new, 8)
    swap = jnp.where(iota((32, 32), 1) == order, 1.0, 0.0).astype(BF16)
    heads = dot(swap, attended.astype(BF16)).reshape(4, 1, 8, 128)
    att_all[:, pl.ds(p, 1)] = heads.astype(BF16)
    for i in range(X):
        for j in range(Y):
            if i or j:
                there = rem(x + i, X) * (2 * Y) + h * Y + rem(y + j, Y)
                send(att_all.at[:, p], att_all.at[:, p], ssem.at[1], rsem.at[1], there, e)

    wait_bytes(wo_ref, early.at[0])
    wait_bytes(att_all.at[:, pl.ds(0, PL - 1)], rsem.at[1])
    rows = jnp.concatenate(
        [att_all[r].astype(F32).reshape(PL * 8, 128) for r in range(4)], axis=1
    ).astype(BF16)
    partial = dot(rows, jnp.concatenate([w_all[0], w_all[1]], axis=1))
    rs_send[...] = partial.reshape(E, PB * 8, 256).astype(BF16)
    rs_recv[pl.ds(e, 1)] = rs_send[pl.ds(e, 1)]

    for i in range(1, E):
        ee = rem(e + i, E)
        send(rs_send.at[ee], rs_recv.at[e], ssem.at[2], rsem.at[2], c, ee)

    for i in range(PB):

        @pl.when(p != e * PB + i)
        def _():
            wait_bytes(res_recv.at[i], early.at[2 + i])
            wait_bytes(g_recv.at[i], early.at[2 + PB + i])

    pick_rows = E * PB * CAP
    table = g_recv[...].reshape(PB * 8, 128).astype(BF16)
    pick = iota((pick_rows, 128), 0)
    chooser = jnp.where(
        iota((pick_rows, 128), 1) == div(pick, PB * CAP) * CAP + rem(pick, CAP), 1.0, 0.0
    ).astype(BF16)
    picks = dot_nt(chooser, table)
    pick = iota((pick_rows, PB * 8), 0)
    picks = jnp.where(
        rem(div(pick, CAP), PB) == div(iota((pick_rows, PB * 8), 1), 8), picks, 0.0
    ).astype(BF16)
    residual = jnp.concatenate(
        [
            jnp.concatenate([res_recv[i, half].astype(F32) for half in range(2)], axis=1)
            for i in range(PB)
        ],
        axis=0,
    )

    wait_bytes(rs_recv.at[pl.ds(0, E - 1)], rsem.at[2])
    stream = residual
    for i in range(E):
        stream = stream + rs_recv[i].astype(F32)
    z_send[...] = dot(picks, stream.astype(BF16)).reshape(E, PB * CAP, 256).astype(BF16)
    xall[pl.ds(p, 1), pl.ds(hz, 1)] = z_send[pl.ds(e, 1)][None]

    for i in range(1, 2 * E):
        zz = rem(hz + i, 2 * E)
        ee = rem(zz, E)
        send(z_send.at[ee], xall.at[p, hz], ssem.at[3], rsem.at[3], at_z(div(zz, E)), ee)

    sq_acc[...] = jnp.zeros_like(sq_acc)
    accg[...] = jnp.zeros_like(accg)
    accu[...] = jnp.zeros_like(accu)
    weights[0].wait()
    weights[1].wait()
    wait_bytes(xall.at[p, pl.ds(0, 2 * E - 1)], rsem.at[3])

    def ctx_of(i, j):
        return rem(x + i, X) * (2 * Y) + h * Y + rem(y + j, Y)

    def source(i, j):
        return rem(x + X - i, X), rem(y + Y - j, Y)

    low_half, high_half = pl.ds(0, E), pl.ds(E, E)

    def expert_products(xx, yy):
        src = xx * Y + yy
        part = xall[src].astype(F32).reshape(S, 256)
        sq_acc[...] += part[:, :128] * part[:, :128] + part[:, 128:] * part[:, 128:]
        low = pl.multiple_of((xx * (2 * Y) + yy) * 128, 128)
        high = pl.multiple_of((xx * (2 * Y) + Y + yy) * 128, 128)
        gain = [gain_ref[pl.ds(xx * (2 * Y) + half * Y + yy, 1), :] for half in range(2)]
        scaled = (part * jnp.concatenate(gain, axis=1)).astype(BF16)
        for acc, w in ((accg, wg_s), (accu, wu_s)):
            block = jnp.concatenate([w[:, pl.ds(low, 128)], w[:, pl.ds(high, 128)]], axis=1)
            acc[...] += dot_nt(scaled, block)
        own = dot(f_sel[...], part.astype(BF16))
        sown[:, pl.ds(low, 128)] = own[:, :128]
        sown[:, pl.ds(high, 128)] = own[:, 128:]

    for i in near_first(max(X, Y)):
        if i < X:
            send(xall.at[p], xall.at[p], ssem.at[4], d_recv.at[i * Y], ctx_of(i, 0), e)
        if i < Y:
            send(xall.at[p], xall.at[p], ssem.at[4], d_recv.at[i], ctx_of(0, i), e)
    expert_products(x, y)
    for i in near_first(max(X, Y)):
        if i < X:
            xx, yy = source(i, 0)
            src = xx * Y + yy
            wait_bytes(xall.at[src], d_recv.at[i * Y])
            for j in near_first(Y):
                half = xall.at[src, low_half]
                send(half, half, ssem.at[4], d_recv.at[i * Y + j], ctx_of(0, j), e)
        if i < Y:
            xx, yy = source(0, i)
            src = xx * Y + yy
            wait_bytes(xall.at[src], d_recv.at[i])
            for j in near_first(X):
                half = xall.at[src, high_half]
                send(half, half, ssem.at[4], d_recv.at[PL + j * Y + i], ctx_of(j, 0), e)

    @pl.loop(1, X)
    def _(i):
        expert_products(*source(i, 0))

    @pl.loop(1, Y)
    def _(i):
        expert_products(*source(0, i))

    @pl.loop(0, (X - 1) * (Y - 1))
    def _(t):
        i, j = div(t, Y - 1) + 1, rem(t, Y - 1) + 1
        xx, yy = source(i, j)
        src = xx * Y + yy
        wait_bytes(xall.at[src, low_half], d_recv.at[i * Y + j])
        wait_bytes(xall.at[src, high_half], d_recv.at[PL + i * Y + j])
        expert_products(xx, yy)

    norm = lax.rsqrt(jnp.sum(sq_acc[...], axis=1, keepdims=True) / D + 1e-05)
    gate_val = accg[...] * norm
    act = ((gate_val / (1.0 + jnp.exp(-gate_val))) * (accu[...] * norm)).astype(BF16)
    new = iota((S, S), 0)
    order = rem(div(new, CAP), 2) * (PL * CAP) + div(new, 2 * CAP) * CAP + rem(new, CAP)
    act = dot(jnp.where(iota((S, S), 1) == order, 1.0, 0.0).astype(BF16), act).astype(BF16)

    weights[2].wait()
    for n in range(NCH):
        down = dot(act, wd_s[:, n * chunk_cols : (n + 1) * chunk_cols])
        e_send[n] = down.reshape(X, Y, 2 * CAP, chunk_cols).astype(BF16)
        if n % 2 == 0:
            for j in near_first(Y):
                block = e_send.at[n, :, rem(y + j, Y)]
                send(block, e_recv.at[n, j - 1, pl.ds(0, X)], ssem.at[5], e_sem.at[n], ctx_of(0, j), e)
        else:
            for i in near_first(X):
                block = e_send.at[n, rem(x + i, X)]
                send(block, e_recv.at[n, i - 1, pl.ds(0, Y)], ssem.at[11], e_sem.at[n], ctx_of(i, 0), e)

    for n in range(NCH):
        if n % 2 == 0:
            wait_bytes(e_recv.at[n, pl.ds(0, Y - 1), pl.ds(0, X)], e_sem.at[n])
            line = e_send[n, :, pl.ds(y, 1)].reshape(X, 2 * CAP, chunk_cols).astype(F32)
            for j in range(Y - 1):
                line = line + e_recv[n, j, :X].astype(F32)
            t_send[n, :X] = line.astype(BF16)
            for i in near_first(X):
                block = t_send.at[n, rem(x + i, X)]
                send(block, t_recv.at[n, i - 1], ssem.at[12], t_sem.at[n], ctx_of(i, 0), e)
        else:
            wait_bytes(e_recv.at[n, pl.ds(0, X - 1), pl.ds(0, Y)], e_sem.at[n])
            line = e_send[n, pl.ds(x, 1)].reshape(Y, 2 * CAP, chunk_cols).astype(F32)
            for i in range(X - 1):
                line = line + e_recv[n, i, :Y].astype(F32)
            t_send[n, :Y] = line.astype(BF16)
            for j in near_first(Y):
                block = t_send.at[n, rem(y + j, Y)]
                send(block, t_recv.at[n, j - 1], ssem.at[13], t_sem.at[n], ctx_of(0, j), e)

    wait_bytes(gg_all.at[h], early.at[1])
    weigh = [
        [
            jnp.sum(jnp.where(lane8 == e * CAP + s, gg_all[hh], 0.0), axis=1, keepdims=True)
            for s in range(CAP)
        ]
        for hh in range(2)
    ]
    for n in range(NCH):
        peers, mine = (X - 1, x) if n % 2 == 0 else (Y - 1, y)
        wait_bytes(t_recv.at[n, pl.ds(0, peers)], t_sem.at[n])
        total = t_send[n, mine].astype(F32)
        for i in range(peers):
            total = total + t_recv[n, i].astype(F32)
        for f in range(chunk_cols // CE):
            ee = n * (chunk_cols // CE) + f
            stream_own = sown[:, ee * CE : (ee + 1) * CE]
            for hh in range(2):
                term = jnp.where(h == hh, stream_own, 0.0)
                for s in range(CAP):
                    line = hh * CAP + s
                    term = term + weigh[hh][s] * total[line : line + 1, f * CE : (f + 1) * CE]
                f_send[hh * E + ee] = term.astype(BF16)
                away = (h != hh) | (e != ee)

                @pl.when(away)
                def _():
                    send(f_send.at[hh * E + ee], f_recv.at[hz], ssem.at[6], rsem.at[4], at_z(hh), ee)

    f_recv[pl.ds(hz, 1)] = f_send[pl.ds(hz, 1)]
    wait_bytes(f_recv.at[pl.ds(0, 2 * E - 1)], rsem.at[4])
    out_ref[...] = jnp.sum(f_recv[...].astype(F32), axis=0).astype(BF16)

    wait_bytes(abuf.at[pl.ds(0, CTX - 1)], ssem.at[0])
    wait_bytes(att_all.at[:, pl.ds(0, PL - 1)], ssem.at[1])
    wait_bytes(rs_send.at[pl.ds(0, E - 1)], ssem.at[2])
    wait_bytes(xall.at[0, pl.ds(0, 2 * E - 1)], ssem.at[3])
    wait_bytes(xall.at[pl.ds(0, PL - 1)], ssem.at[4])
    even, odd = pl.ds(0, (NCH + 1) // 2), pl.ds(0, NCH // 2)
    wait_bytes(e_send.at[even, :, pl.ds(0, Y - 1)], ssem.at[5])
    wait_bytes(e_send.at[odd, pl.ds(0, X - 1)], ssem.at[11])
    wait_bytes(t_send.at[even, pl.ds(0, X - 1)], ssem.at[12])
    wait_bytes(t_send.at[odd, pl.ds(0, Y - 1)], ssem.at[13])
    wait_bytes(f_send.at[pl.ds(0, 2 * E - 1)], ssem.at[6])
    wait_bytes(wo_ref, ssem.at[7])
    wait_bytes(gg_all.at[h], ssem.at[8])

    @pl.when(spread)
    def _():
        wait_bytes(f_recv.at[pl.ds(0, PL - 1), :, pl.ds(0, 256)], ssem.at[9])
        wait_bytes(f_recv.at[pl.ds(0, PL - 1), :, pl.ds(0, 256)], ssem.at[10])


def local(queries, keys, values, out_proj, residual, gain, routes, gates, w_gate, w_up, w_down):
    X, Y = PLANE
    CTX, PL, E = 2 * X * Y, X * Y, lax.axis_size("exp")
    PB, D, FF = PL // E, gain.shape[0], w_gate.shape[2]
    S, CE = 2 * PL * CAP, D // E
    chunk_cols, side = 1024, max(X, Y)
    NCH = D // chunk_cols
    vmem = pl.BlockSpec(memory_space=pltpu.VMEM)
    return pl.pallas_call(
        functools.partial(kernel, (X, Y, E, chunk_cols)),
        out_shape=jax.ShapeDtypeStruct((8, CE), BF16),
        in_specs=[vmem] * 8 + [pl.BlockSpec(memory_space=pl.ANY)] * 3,
        out_specs=vmem,
        scratch_shapes=[
            pltpu.VMEM((CTX, 40, 128), BF16),
            pltpu.VMEM((CTX, 40, 128), BF16),
            pltpu.VMEM((128, 128), F32),
            pltpu.VMEM((4, PL, 8, 128), BF16),
            pltpu.VMEM((2, 512, 128), BF16),
            pltpu.VMEM((E, PB * 8, 256), BF16),
            pltpu.VMEM((E, PB * 8, 256), BF16),
            pltpu.VMEM((PB, 2, 8, 128), BF16),
            pltpu.VMEM((8, 128), F32),
            pltpu.VMEM((PB, 8, 128), F32),
            pltpu.VMEM((2, 8, 128), F32),
            pltpu.VMEM((8, S), BF16),
            pltpu.VMEM((E, PB * CAP, 256), BF16),
            pltpu.VMEM((PL, 2 * E, PB * CAP, 256), BF16),
            pltpu.VMEM((S, 128), F32),
            pltpu.VMEM((S, FF), F32),
            pltpu.VMEM((S, FF), F32),
            pltpu.VMEM((8, D), F32),
            pltpu.VMEM((NCH, X, Y, 2 * CAP, chunk_cols), BF16),
            pltpu.VMEM((NCH, side - 1, side, 2 * CAP, chunk_cols), BF16),
            pltpu.VMEM((NCH, side, 2 * CAP, chunk_cols), BF16),
            pltpu.VMEM((NCH, side - 1, 2 * CAP, chunk_cols), BF16),
            pltpu.VMEM((2 * E, 8, CE), BF16),
            pltpu.VMEM((2 * E, 8, CE), BF16),
            pltpu.VMEM((FF, D), BF16),
            pltpu.VMEM((FF, D), BF16),
            pltpu.VMEM((FF, D), BF16),
            pltpu.SemaphoreType.DMA((3,)),
            pltpu.SemaphoreType.DMA((14,)),
            pltpu.SemaphoreType.DMA((5,)),
            pltpu.SemaphoreType.DMA((2 + 2 * PB,)),
            pltpu.SemaphoreType.DMA((2 * PL,)),
            pltpu.SemaphoreType.DMA((NCH,)),
            pltpu.SemaphoreType.DMA((NCH,)),
        ],
        compiler_params=pltpu.CompilerParams(
            collective_id=0, has_side_effects=True, vmem_limit_bytes=VMEM_LIMIT
        ),
    )(
        queries.reshape(CTX * 32, 128),
        keys.reshape(keys.shape[0], 128),
        values.reshape(values.shape[0], 128),
        out_proj,
        residual,
        gain.reshape(CTX, 128),
        routes.T,
        gates.T,
        jnp.swapaxes(w_gate, 1, 2).reshape(FF, D),
        jnp.swapaxes(w_up, 1, 2).reshape(FF, D),
        w_down.reshape(FF, D),
    )


def solution(mesh):
    return jax.shard_map(
        local,
        mesh=mesh,
        in_specs=(
            P(None, "exp", None),
            P("ctx", "exp", None),
            P("ctx", "exp", None),
            P("exp", "ctx"),
            P("ctx", None),
            P(),
            P("ctx", None),
            P("ctx", None),
            P("exp", None, "ctx"),
            P("exp", None, "ctx"),
            P("exp", "ctx", None),
        ),
        out_specs=P("ctx", "exp"),
        check_vma=False,
    )
```

```python
import functools
import math

import jax
import jax.numpy as jnp
from jax import lax
from jax.experimental import pallas as pl
from jax.experimental.pallas import tpu as pltpu
from jax.sharding import PartitionSpec as P

F32 = jnp.float32
BF16 = jnp.bfloat16
PLANE = (4, 4)
CAP = 4
VMEM_LIMIT = 56 * 1024 * 1024


def iota(shape, dim):
    return lax.broadcasted_iota(jnp.int32, shape, dim)


def div(a, b):
    return lax.div(a, jnp.int32(b))


def rem(a, b):
    return lax.rem(a, jnp.int32(b))


def parts(a, n):
    assert n & (n - 1) == 0
    return lax.shift_right_logical(a, jnp.int32(n.bit_length() - 1)), a & (n - 1)


def dot(a, b):
    return lax.dot_general(a, b, (((1,), (0,)), ((), ())), preferred_element_type=F32)


def dot_nt(a, b):
    return lax.dot_general(a, b, (((1,), (1,)), ((), ())), preferred_element_type=F32)


def near_first(n):
    return sorted(range(1, n), key=lambda i: min(i, n - i))


def wait_bytes(ref, sem):
    pltpu.make_async_copy(ref, ref, sem).wait()


def kernel(
    geom,
    q_hbm, k_hbm, v_hbm, wo_hbm, res_hbm, gain_hbm, routes_hbm, gates_hbm, wg_hbm, wu_hbm, wd_hbm,
    out_hbm,
    out_s, q_ref, k_ref, v_ref, res_ref, gain_ref, routes_ref, gates_ref, swap_s, order_s, picks_s, mask_s,
    abuf, arecv, a_out, a_in, wt_s, att_all, w_all, rs_send, rs_recv, res_recv, g_own, g_recv, gg_all, f_sel,
    z_send, xall, sq_acc, accg, accu, sown, e_send, e_recv, t_send, t_recv, f_send, f_recv,
    wg_s, wu_s, wd_s,
    wsem, ssem, a_sem, rsem, early, d_recv, e_sem, t_sem,
):
    X, Y, E, chunk_cols = geom
    PL, CTX = X * Y, 2 * X * Y
    PB = PL // E
    D = CTX * 128
    S = 2 * PL * CAP
    NCH, CE = D // chunk_cols, D // E
    tokens = CTX * 8
    key_rows = k_ref.shape[0]

    c = lax.axis_index("ctx")
    e = lax.axis_index("exp")
    x = div(c, 2 * Y)
    h = rem(div(c, Y), 2)
    y = rem(c, Y)
    p = x * Y + y
    hz = h * E + e

    def at_plane(pp):
        return div(pp, Y) * (2 * Y) + h * Y + rem(pp, Y)

    def at_z(hh):
        return x * (2 * Y) + hh * Y + y

    def send(src, dst, ssem_, rsem_, ctx, exp):
        pltpu.make_async_remote_copy(
            src_ref=src, dst_ref=dst, send_sem=ssem_, recv_sem=rsem_,
            device_id={"ctx": ctx, "exp": exp}, device_id_type=pl.DeviceIdType.MESH,
        ).start()

    barrier = pltpu.get_barrier_semaphore()

    for i in range(X):
        for hh in range(2):
            for j in range(Y):
                there = rem(x + i, X) * (2 * Y) + rem(h + hh, 2) * Y + rem(y + j, Y)
                if i or hh or j:
                    pl.semaphore_signal(
                        barrier, inc=1, device_id={"ctx": there, "exp": e},
                        device_id_type=pl.DeviceIdType.MESH,
                    )
    for i in range(1, E):
        for hh in range(2):
            pl.semaphore_signal(
                barrier, inc=1, device_id={"ctx": at_z(hh), "exp": rem(e + i, E)},
                device_id_type=pl.DeviceIdType.MESH,
            )

    fetches = [
        pltpu.make_async_copy(a, b, wsem.at[i])
        for i, (a, b) in enumerate((
            (wg_hbm, wg_s), (wu_hbm, wu_s), (wd_hbm, wd_s),
            (q_hbm, q_ref), (k_hbm, k_ref), (v_hbm, v_ref), (routes_hbm, routes_ref),
            (gates_hbm, gates_ref), (res_hbm, res_ref), (gain_hbm, gain_ref), (wo_hbm, w_all.at[h]),
        ))
    ]
    for i in (6, 7, 3, 4, 5, 8, 9, 10, 0, 1, 2):
        fetches[i].start()
    weights = fetches[:3]

    new, old = iota((32, 32), 0), iota((32, 32), 1)
    head, token = parts(new, 8)
    swap_s[...] = jnp.where(old == token * 4 + head, 1.0, 0.0).astype(BF16)
    high, s4 = parts(iota((S, S), 0), CAP)
    plane, zz = parts(high, 2)
    order_s[...] = jnp.where(
        iota((S, S), 1) == zz * (PL * CAP) + plane * CAP + s4, 1.0, 0.0
    ).astype(BF16)
    pick_rows = E * PB * CAP
    high, s4 = parts(iota((pick_rows, 128), 0), CAP)
    picks_s[...] = jnp.where(
        iota((pick_rows, 128), 1) == parts(high, PB)[0] * CAP + s4, 1.0, 0.0
    ).astype(BF16)
    high, _ = parts(iota((pick_rows, PB * 8), 0), CAP)
    mask_s[...] = jnp.where(
        parts(high, PB)[1] == parts(iota((pick_rows, PB * 8), 1), 8)[0], 1.0, 0.0
    )
    fetches[6].wait()
    fetches[7].wait()

    lane8 = iota((8, 128), 1)
    row8 = iota((8, 128), 0)
    diagonal = iota((8, 8), 0) == iota((8, 8), 1)
    route = [
        jnp.sum(
            jnp.where(diagonal, routes_ref[k : k + 1, :].astype(F32), 0.0), axis=1, keepdims=True
        ).astype(jnp.int32)
        for k in range(2)
    ]
    gate = [
        jnp.sum(jnp.where(diagonal, gates_ref[k : k + 1, :], 0.0), axis=1, keepdims=True)
        for k in range(2)
    ]
    hit = jnp.where((lane8 == route[0]) | (lane8 == route[1]), 1.0, 0.0)
    before = jnp.zeros((8, 128), F32)
    for t in range(7):
        before = before + jnp.where(row8 > t, hit[t : t + 1, :], 0.0)
    slot = [
        jnp.sum(jnp.where(lane8 == route[k], before, 0.0), axis=1, keepdims=True).astype(jnp.int32)
        for k in range(2)
    ]
    place = [route[k] * CAP + slot[k] for k in range(2)]
    g_own[...] = jnp.where((lane8 == place[0]) | (lane8 == place[1]), 1.0, 0.0)
    own_gates = jnp.where(lane8 == place[0], gate[0], 0.0) + jnp.where(
        lane8 == place[1], gate[1], 0.0
    )
    gg_all[pl.ds(h, 1)] = own_gates[None]
    row_s = iota((8, S), 1)
    high, s4 = parts(row_s, CAP)
    f_sel[...] = jnp.where(
        (high == h * PL + p) & (route[0] == e) & (slot[0] == s4), 1.0, 0.0
    ).astype(BF16)

    scale = 1.0 / math.sqrt(128)
    tail = key_rows - min(tokens, key_rows)

    def level_lines(flat):
        hi = flat.astype(BF16).astype(F32)
        mid = (flat - hi).astype(BF16).astype(F32)
        lo = flat - hi - mid
        return jnp.where(
            row8 == 0, hi, jnp.where(row8 == 1, mid, jnp.where(row8 == 2, lo, 0.0))
        ).astype(BF16)

    def attend(j):
        q = q_ref[pl.ds(pl.multiple_of(j * 128, 128), 128), :]
        s = dot_nt(q, k_ref[...]) * scale
        token = j * 32 + parts(iota((128, key_rows - tail), 0), 4)[0]
        limit = (CTX * key_rows - tokens) - c * key_rows + token
        masked = jnp.where(
            tail + iota((128, key_rows - tail), 1) <= limit, s[:, tail:], jnp.float32(-1e30)
        )
        s = jnp.concatenate([s[:, :tail], masked], axis=1) if tail else masked
        m = jnp.max(s, axis=1, keepdims=True)
        w = jnp.exp(s - m)
        total = jnp.sum(w, axis=1, keepdims=True)
        o = (dot(w.astype(BF16), v_ref[...]) / total).astype(BF16)
        lse = m + jnp.log(total)
        flat = jnp.sum(
            jnp.where(iota((128, 128), 0) == iota((128, 128), 1), lse, 0.0), axis=0, keepdims=True
        )
        lines = level_lines(flat)
        for r in range(4):
            abuf[j * 4 + r, 0:32, :] = o[r * 32 : (r + 1) * 32, :]
            abuf[j * 4 + r, 32:40, :] = lines

    for i in (3, 4, 5):
        fetches[i].wait()

    @pl.loop(0, CTX // 4)
    def _(j):
        attend(j)

    other = at_z(1 - h)
    arecv[0, pl.ds(p, 1)] = abuf[pl.ds(c, 1)]
    arecv[1, pl.ds(p, 1)] = abuf[pl.ds(other, 1)]
    for i in (8, 9, 10):
        fetches[i].wait()
    pl.semaphore_wait(barrier, CTX - 1 + 2 * (E - 1))

    send(w_all.at[h], w_all.at[h], ssem.at[7], early.at[0], other, e)

    far_first = sorted(
        ((i, j) for i in range(X) for j in range(Y)),
        key=lambda d: -min(d[0], X - d[0]) - min(d[1], Y - d[1]),
    )
    for hh in (1, 0):
        for i, j in far_first:
            if i or j:
                there = rem(x + i, X) * (2 * Y) + rem(y + j, Y)
                block = there + rem(h + hh, 2) * Y
                send(abuf.at[block], arecv.at[hh, p], ssem.at[0], a_sem.at[hh], there + h * Y, e)

    send(gg_all.at[h], gg_all.at[h], ssem.at[8], early.at[1], at_z(1 - h), e)
    spread = div(p, PB) == e
    mine = rem(p, PB)

    @pl.when(spread)
    def _():
        @pl.loop(1, PL)
        def _(i):
            pp = rem(p + i, PL)
            there = at_plane(pp)
            low = div(pp, Y) * (2 * Y) + rem(pp, Y)
            for half in range(2):
                cols = pl.ds(pl.multiple_of((low + half * Y) * 128, 128), 128)
                send(res_ref.at[:, cols], res_recv.at[mine, half], ssem.at[9], early.at[2 + mine], there, e)
            send(g_own, g_recv.at[mine], ssem.at[10], early.at[2 + PB + mine], there, e)

        low = x * (2 * Y) + y
        for half in range(2):
            cols = pl.ds(pl.multiple_of((low + half * Y) * 128, 128), 128)
            res_recv[pl.ds(mine, 1), half] = res_ref[:, cols][None]
        g_recv[pl.ds(mine, 1)] = g_own[...][None]

    def combine(pairs, block):
        levels = jnp.full((32, 128), -1e30, F32)
        for i, (_, lines) in enumerate(pairs):
            line = jnp.sum(lines(), axis=0, keepdims=True)
            levels = jnp.where(iota((32, 128), 0) == i, line, levels)
        top = jnp.max(levels, axis=0, keepdims=True)
        weight = jnp.exp(levels - top)
        total = jnp.sum(weight, axis=0, keepdims=True)
        weight = jnp.concatenate([weight / total, jnp.zeros((96, 128), F32)], axis=0)
        wt_s[...] = weight.T
        columns = wt_s[pl.ds(pl.multiple_of(rem(block, 4) * 32, 32), 32), :]
        attended = jnp.zeros((32, 128), F32)
        for i, (rows, _) in enumerate(pairs):
            attended = attended + rows() * columns[:, i : i + 1]
        return attended, top + jnp.log(total)

    def slab(ref, *at):
        return (
            lambda: ref[(*at, slice(0, 32))].astype(F32),
            lambda: ref[(*at, slice(32, 40))].astype(F32),
        )

    wait_bytes(arecv.at[1, pl.ds(0, PL - 1)], a_sem.at[1])
    attended, level = combine([slab(arecv, 1, i) for i in range(PL)], other)
    a_out[0:32, :] = attended.astype(BF16)
    a_out[32:40, :] = level_lines(level)
    send(a_out, a_in, ssem.at[14], early.at[2 + 2 * PB], other, e)

    wait_bytes(arecv.at[0, pl.ds(0, PL - 1)], a_sem.at[0])
    own_part, own_level = combine([slab(arecv, 0, i) for i in range(PL)], c)
    own_lines = jnp.where(row8 == 0, own_level, 0.0)
    wait_bytes(a_in, early.at[2 + 2 * PB])
    attended, _ = combine([(lambda: own_part, lambda: own_lines), slab(a_in)], c)
    heads = dot(swap_s[...], attended.astype(BF16)).reshape(4, 1, 8, 128)
    att_all[:, pl.ds(p, 1)] = heads.astype(BF16)
    for i, j in far_first:
        if i or j:
            there = rem(x + i, X) * (2 * Y) + h * Y + rem(y + j, Y)
            send(att_all.at[:, p], att_all.at[:, p], ssem.at[1], rsem.at[1], there, e)

    wait_bytes(w_all.at[h], early.at[0])
    wait_bytes(att_all.at[:, pl.ds(0, PL - 1)], rsem.at[1])
    rows = jnp.concatenate(
        [att_all[r].astype(F32).reshape(PL * 8, 128) for r in range(4)], axis=1
    ).astype(BF16)
    partial = dot(rows, jnp.concatenate([w_all[0], w_all[1]], axis=1))
    rs_send[...] = partial.reshape(E, PB * 8, 256).astype(BF16)
    rs_recv[pl.ds(e, 1)] = rs_send[pl.ds(e, 1)]

    for i in sorted(range(1, E), key=lambda i: abs(i - E // 2)):
        ee = rem(e + i, E)
        send(rs_send.at[ee], rs_recv.at[e], ssem.at[2], rsem.at[2], c, ee)

    for i in range(PB):

        @pl.when(p != e * PB + i)
        def _():
            wait_bytes(res_recv.at[i], early.at[2 + i])
            wait_bytes(g_recv.at[i], early.at[2 + PB + i])

    table = g_recv[...].reshape(PB * 8, 128).astype(BF16)
    picks = (dot_nt(picks_s[...], table) * mask_s[...]).astype(BF16)
    residual = jnp.concatenate(
        [
            jnp.concatenate([res_recv[i, half].astype(F32) for half in range(2)], axis=1)
            for i in range(PB)
        ],
        axis=0,
    )

    wait_bytes(rs_recv.at[pl.ds(0, E - 1)], rsem.at[2])
    stream = residual
    for i in range(E):
        stream = stream + rs_recv[i].astype(F32)
    z_send[...] = dot(picks, stream.astype(BF16)).reshape(E, PB * CAP, 256).astype(BF16)
    xall[pl.ds(p, 1), pl.ds(hz, 1)] = z_send[pl.ds(e, 1)][None]

    for i in sorted(range(1, 2 * E), key=lambda i: abs(i - E)):
        zz = rem(hz + i, 2 * E)
        ee = rem(zz, E)
        send(z_send.at[ee], xall.at[p, hz], ssem.at[3], rsem.at[3], at_z(div(zz, E)), ee)

    sq_acc[...] = jnp.zeros_like(sq_acc)
    accg[...] = jnp.zeros_like(accg)
    accu[...] = jnp.zeros_like(accu)
    weights[0].wait()
    weights[1].wait()
    wait_bytes(xall.at[p, pl.ds(0, 2 * E - 1)], rsem.at[3])

    def ctx_of(i, j):
        return rem(x + i, X) * (2 * Y) + h * Y + rem(y + j, Y)

    def source(i, j):
        return rem(x + X - i, X), rem(y + Y - j, Y)

    low_half, high_half = pl.ds(0, E), pl.ds(E, E)

    def expert_products(xx, yy):
        src = xx * Y + yy
        part = xall[src].astype(F32).reshape(S, 256)
        sq_acc[...] += part[:, :128] * part[:, :128] + part[:, 128:] * part[:, 128:]
        low = pl.multiple_of((xx * (2 * Y) + yy) * 128, 128)
        high = pl.multiple_of((xx * (2 * Y) + Y + yy) * 128, 128)
        gain = [gain_ref[pl.ds(xx * (2 * Y) + half * Y + yy, 1), :] for half in range(2)]
        scaled = (part * jnp.concatenate(gain, axis=1)).astype(BF16)
        for acc, w in ((accg, wg_s), (accu, wu_s)):
            block = jnp.concatenate([w[:, pl.ds(low, 128)], w[:, pl.ds(high, 128)]], axis=1)
            acc[...] += dot_nt(scaled, block)
        own = dot(f_sel[...], part.astype(BF16))
        sown[:, pl.ds(low, 128)] = own[:, :128]
        sown[:, pl.ds(high, 128)] = own[:, 128:]

    for i in near_first(max(X, Y)):
        if i < X:
            send(xall.at[p], xall.at[p], ssem.at[4], d_recv.at[i * Y], ctx_of(i, 0), e)
        if i < Y:
            send(xall.at[p], xall.at[p], ssem.at[4], d_recv.at[i], ctx_of(0, i), e)
    expert_products(x, y)
    def forward(i, j):
        xx, yy = source(i, j)
        src = xx * Y + yy
        wait_bytes(xall.at[src], d_recv.at[i * Y + j])
        if i:
            half = xall.at[src, low_half]
            for n in near_first(Y):
                send(half, half, ssem.at[4], d_recv.at[i * Y + n], ctx_of(0, n), e)
        else:
            half = xall.at[src, high_half]
            for n in near_first(X):
                send(half, half, ssem.at[4], d_recv.at[PL + n * Y + j], ctx_of(n, 0), e)

    def is_near(d):
        return min(d[0], X - d[0]) + min(d[1], Y - d[1]) == 1

    direct = [(i, 0) for i in range(1, X)] + [(0, j) for j in range(1, Y)]
    for group in ([d for d in direct if is_near(d)], [d for d in direct if not is_near(d)]):
        for i, j in group:
            forward(i, j)
        for i, j in group:
            expert_products(*source(i, j))

    @pl.loop(0, (X - 1) * (Y - 1))
    def _(t):
        i, j = div(t, Y - 1) + 1, rem(t, Y - 1) + 1
        xx, yy = source(i, j)
        src = xx * Y + yy
        wait_bytes(xall.at[src, low_half], d_recv.at[i * Y + j])
        wait_bytes(xall.at[src, high_half], d_recv.at[PL + i * Y + j])
        expert_products(xx, yy)

    norm = lax.rsqrt(jnp.sum(sq_acc[...], axis=1, keepdims=True) / D + 1e-05)
    gate_val = accg[...] * norm
    act = ((gate_val / (1.0 + jnp.exp(-gate_val))) * (accu[...] * norm)).astype(BF16)
    act = dot(order_s[...], act).astype(BF16)

    weights[2].wait()
    for n in range(NCH):
        down = dot(act, wd_s[:, n * chunk_cols : (n + 1) * chunk_cols])
        e_send[n] = down.reshape(X, Y, 2 * CAP, chunk_cols).astype(BF16)
        if n % 2 == 0:
            for j in near_first(Y):
                block = e_send.at[n, :, rem(y + j, Y)]
                send(block, e_recv.at[n, j - 1, pl.ds(0, X)], ssem.at[5], e_sem.at[n], ctx_of(0, j), e)
        else:
            for i in near_first(X):
                block = e_send.at[n, rem(x + i, X)]
                send(block, e_recv.at[n, i - 1, pl.ds(0, Y)], ssem.at[11], e_sem.at[n], ctx_of(i, 0), e)

    for n in range(NCH):
        if n % 2 == 0:
            wait_bytes(e_recv.at[n, pl.ds(0, Y - 1), pl.ds(0, X)], e_sem.at[n])
            line = e_send[n, :, pl.ds(y, 1)].reshape(X, 2 * CAP, chunk_cols).astype(F32)
            for j in range(Y - 1):
                line = line + e_recv[n, j, :X].astype(F32)
            t_send[n, :X] = line.astype(BF16)
            for i in near_first(X):
                block = t_send.at[n, rem(x + i, X)]
                send(block, t_recv.at[n, i - 1], ssem.at[12], t_sem.at[n], ctx_of(i, 0), e)
        else:
            wait_bytes(e_recv.at[n, pl.ds(0, X - 1), pl.ds(0, Y)], e_sem.at[n])
            line = e_send[n, pl.ds(x, 1)].reshape(Y, 2 * CAP, chunk_cols).astype(F32)
            for i in range(X - 1):
                line = line + e_recv[n, i, :Y].astype(F32)
            t_send[n, :Y] = line.astype(BF16)
            for j in near_first(Y):
                block = t_send.at[n, rem(y + j, Y)]
                send(block, t_recv.at[n, j - 1], ssem.at[13], t_sem.at[n], ctx_of(0, j), e)

    wait_bytes(gg_all.at[h], early.at[1])
    weigh = [
        [
            jnp.sum(jnp.where(lane8 == e * CAP + s, gg_all[hh], 0.0), axis=1, keepdims=True)
            for s in range(CAP)
        ]
        for hh in range(2)
    ]
    for n in range(NCH):
        peers, mine = (X - 1, x) if n % 2 == 0 else (Y - 1, y)
        wait_bytes(t_recv.at[n, pl.ds(0, peers)], t_sem.at[n])
        total = t_send[n, mine].astype(F32)
        for i in range(peers):
            total = total + t_recv[n, i].astype(F32)
        for f in range(chunk_cols // CE):
            ee = n * (chunk_cols // CE) + f
            stream_own = sown[:, ee * CE : (ee + 1) * CE]
            for hh in range(2):
                term = jnp.where(h == hh, stream_own, 0.0)
                for s in range(CAP):
                    line = hh * CAP + s
                    term = term + weigh[hh][s] * total[line : line + 1, f * CE : (f + 1) * CE]
                f_send[hh * E + ee] = term.astype(BF16)
                away = (h != hh) | (e != ee)

                @pl.when(away)
                def _():
                    send(f_send.at[hh * E + ee], f_recv.at[hz], ssem.at[6], rsem.at[4], at_z(hh), ee)

    f_recv[pl.ds(hz, 1)] = f_send[pl.ds(hz, 1)]
    wait_bytes(f_recv.at[pl.ds(0, 2 * E - 1)], rsem.at[4])
    out_s[...] = jnp.sum(f_recv[...].astype(F32), axis=0).astype(BF16)
    result = pltpu.make_async_copy(out_s, out_hbm, wsem.at[0])
    result.start()

    wait_bytes(abuf.at[pl.ds(0, 2 * (PL - 1))], ssem.at[0])
    wait_bytes(a_out, ssem.at[14])
    wait_bytes(att_all.at[:, pl.ds(0, PL - 1)], ssem.at[1])
    wait_bytes(rs_send.at[pl.ds(0, E - 1)], ssem.at[2])
    wait_bytes(xall.at[0, pl.ds(0, 2 * E - 1)], ssem.at[3])
    wait_bytes(xall.at[pl.ds(0, PL - 1)], ssem.at[4])
    even, odd = pl.ds(0, (NCH + 1) // 2), pl.ds(0, NCH // 2)
    wait_bytes(e_send.at[even, :, pl.ds(0, Y - 1)], ssem.at[5])
    wait_bytes(e_send.at[odd, pl.ds(0, X - 1)], ssem.at[11])
    wait_bytes(t_send.at[even, pl.ds(0, X - 1)], ssem.at[12])
    wait_bytes(t_send.at[odd, pl.ds(0, Y - 1)], ssem.at[13])
    wait_bytes(f_send.at[pl.ds(0, 2 * E - 1)], ssem.at[6])
    wait_bytes(w_all.at[h], ssem.at[7])
    wait_bytes(gg_all.at[h], ssem.at[8])

    @pl.when(spread)
    def _():
        wait_bytes(f_recv.at[pl.ds(0, PL - 1), :, pl.ds(0, 256)], ssem.at[9])
        wait_bytes(f_recv.at[pl.ds(0, PL - 1), :, pl.ds(0, 256)], ssem.at[10])
    result.wait()


def local(queries, keys, values, out_proj, residual, gain, routes, gates, w_gate, w_up, w_down):
    X, Y = PLANE
    CTX, PL, E = 2 * X * Y, X * Y, lax.axis_size("exp")
    PB, D, FF = PL // E, gain.shape[0], w_gate.shape[2]
    S, CE = 2 * PL * CAP, D // E
    chunk_cols, side = 512, max(X, Y)
    NCH = D // chunk_cols
    return pl.pallas_call(
        functools.partial(kernel, (X, Y, E, chunk_cols)),
        out_shape=jax.ShapeDtypeStruct((8, CE), BF16),
        in_specs=[pl.BlockSpec(memory_space=pl.ANY)] * 11,
        out_specs=pl.BlockSpec(memory_space=pl.ANY),
        scratch_shapes=[
            pltpu.VMEM((8, CE), BF16),
            pltpu.VMEM((CTX * 32, 128), BF16),
            pltpu.VMEM((keys.shape[0], 128), BF16),
            pltpu.VMEM((keys.shape[0], 128), BF16),
            pltpu.VMEM((8, D), BF16),
            pltpu.VMEM((CTX, 128), F32),
            pltpu.VMEM((2, 8), jnp.int32),
            pltpu.VMEM((2, 8), F32),
            pltpu.VMEM((32, 32), BF16),
            pltpu.VMEM((S, S), BF16),
            pltpu.VMEM((E * PB * CAP, 128), BF16),
            pltpu.VMEM((E * PB * CAP, PB * 8), F32),
            pltpu.VMEM((CTX, 40, 128), BF16),
            pltpu.VMEM((2, PL, 40, 128), BF16),
            pltpu.VMEM((40, 128), BF16),
            pltpu.VMEM((40, 128), BF16),
            pltpu.VMEM((128, 128), F32),
            pltpu.VMEM((4, PL, 8, 128), BF16),
            pltpu.VMEM((2, 512, 128), BF16),
            pltpu.VMEM((E, PB * 8, 256), BF16),
            pltpu.VMEM((E, PB * 8, 256), BF16),
            pltpu.VMEM((PB, 2, 8, 128), BF16),
            pltpu.VMEM((8, 128), F32),
            pltpu.VMEM((PB, 8, 128), F32),
            pltpu.VMEM((2, 8, 128), F32),
            pltpu.VMEM((8, S), BF16),
            pltpu.VMEM((E, PB * CAP, 256), BF16),
            pltpu.VMEM((PL, 2 * E, PB * CAP, 256), BF16),
            pltpu.VMEM((S, 128), F32),
            pltpu.VMEM((S, FF), F32),
            pltpu.VMEM((S, FF), F32),
            pltpu.VMEM((8, D), F32),
            pltpu.VMEM((NCH, X, Y, 2 * CAP, chunk_cols), BF16),
            pltpu.VMEM((NCH, side - 1, side, 2 * CAP, chunk_cols), BF16),
            pltpu.VMEM((NCH, side, 2 * CAP, chunk_cols), BF16),
            pltpu.VMEM((NCH, side - 1, 2 * CAP, chunk_cols), BF16),
            pltpu.VMEM((2 * E, 8, CE), BF16),
            pltpu.VMEM((2 * E, 8, CE), BF16),
            pltpu.VMEM((FF, D), BF16),
            pltpu.VMEM((FF, D), BF16),
            pltpu.VMEM((FF, D), BF16),
            pltpu.SemaphoreType.DMA((11,)),
            pltpu.SemaphoreType.DMA((15,)),
            pltpu.SemaphoreType.DMA((2,)),
            pltpu.SemaphoreType.DMA((5,)),
            pltpu.SemaphoreType.DMA((3 + 2 * PB,)),
            pltpu.SemaphoreType.DMA((2 * PL,)),
            pltpu.SemaphoreType.DMA((NCH,)),
            pltpu.SemaphoreType.DMA((NCH,)),
        ],
        compiler_params=pltpu.CompilerParams(
            collective_id=0, has_side_effects=True, vmem_limit_bytes=VMEM_LIMIT
        ),
    )(
        queries.reshape(CTX * 32, 128),
        keys.reshape(keys.shape[0], 128),
        values.reshape(values.shape[0], 128),
        out_proj,
        residual,
        gain.reshape(CTX, 128),
        routes.T,
        gates.T,
        jnp.swapaxes(w_gate, 1, 2).reshape(FF, D),
        jnp.swapaxes(w_up, 1, 2).reshape(FF, D),
        w_down.reshape(FF, D),
    )


def solution(mesh):
    return jax.shard_map(
        local,
        mesh=mesh,
        in_specs=(
            P(None, "exp", None),
            P("ctx", "exp", None),
            P("ctx", "exp", None),
            P("exp", "ctx"),
            P("ctx", None),
            P(),
            P("ctx", None),
            P("ctx", None),
            P("exp", None, "ctx"),
            P("exp", None, "ctx"),
            P("exp", "ctx", None),
        ),
        out_specs=P("ctx", "exp"),
        check_vma=False,
    )
```

```python
import functools
import math

import jax
import jax.numpy as jnp
from jax import lax
from jax.experimental import pallas as pl
from jax.experimental.pallas import tpu as pltpu
from jax.sharding import PartitionSpec as P

F32 = jnp.float32
BF16 = jnp.bfloat16
PLANE = (4, 4)
CAP = 4
VMEM_LIMIT = 56 * 1024 * 1024


def iota(shape, dim):
    return lax.broadcasted_iota(jnp.int32, shape, dim)


def div(a, b):
    return lax.div(a, jnp.int32(b))


def rem(a, b):
    return lax.rem(a, jnp.int32(b))


def parts(a, n):
    assert n & (n - 1) == 0
    return lax.shift_right_logical(a, jnp.int32(n.bit_length() - 1)), a & (n - 1)


def dot(a, b):
    return lax.dot_general(a, b, (((1,), (0,)), ((), ())), preferred_element_type=F32)


def dot_nt(a, b):
    return lax.dot_general(a, b, (((1,), (1,)), ((), ())), preferred_element_type=F32)


def near_first(n):
    return sorted(range(1, n), key=lambda i: min(i, n - i))


def wait_bytes(ref, sem):
    pltpu.make_async_copy(ref, ref, sem).wait()


def kernel(
    geom,
    q_hbm, k_hbm, v_hbm, wo_hbm, res_hbm, gain_hbm, routes_hbm, gates_hbm, wg_hbm, wu_hbm, wd_hbm,
    out_hbm,
    out_s, q_ref, k_ref, v_ref, res_ref, gain_ref, routes_ref, gates_ref, swap_s, order_s, picks_s, mask_s,
    abuf, arecv, a_out, a_in, wt_s, att_all, w_all, rs_send, rs_recv, res_recv, g_own, g_recv, gg_all, f_sel,
    z_send, xall, sq_acc, accg, accu, sown, e_send, e_recv, t_send, t_recv, f_send, f_recv,
    wg_s, wu_s, wd_s,
    wsem, ssem, a_sem, z_sem, rsem, early, d_recv, e_sem, t_sem,
):
    X, Y, E, chunk_cols = geom
    PL, CTX = X * Y, 2 * X * Y
    PB = PL // E
    D = CTX * 128
    S = 2 * PL * CAP
    NCH, CE = D // chunk_cols, D // E
    tokens = CTX * 8
    key_rows = k_ref.shape[0]

    c = lax.axis_index("ctx")
    e = lax.axis_index("exp")
    x = div(c, 2 * Y)
    h = rem(div(c, Y), 2)
    y = rem(c, Y)
    p = x * Y + y
    hz = h * E + e

    def at_plane(pp):
        return div(pp, Y) * (2 * Y) + h * Y + rem(pp, Y)

    def at_z(hh):
        return x * (2 * Y) + hh * Y + y

    def send(src, dst, ssem_, rsem_, ctx, exp):
        pltpu.make_async_remote_copy(
            src_ref=src, dst_ref=dst, send_sem=ssem_, recv_sem=rsem_,
            device_id={"ctx": ctx, "exp": exp}, device_id_type=pl.DeviceIdType.MESH,
        ).start()

    barrier = pltpu.get_barrier_semaphore()

    for i in range(X):
        for hh in range(2):
            for j in range(Y):
                there = rem(x + i, X) * (2 * Y) + rem(h + hh, 2) * Y + rem(y + j, Y)
                if i or hh or j:
                    pl.semaphore_signal(
                        barrier, inc=1, device_id={"ctx": there, "exp": e},
                        device_id_type=pl.DeviceIdType.MESH,
                    )
    for i in range(1, E):
        for hh in range(2):
            pl.semaphore_signal(
                barrier, inc=1, device_id={"ctx": at_z(hh), "exp": rem(e + i, E)},
                device_id_type=pl.DeviceIdType.MESH,
            )

    fetches = [
        pltpu.make_async_copy(a, b, wsem.at[i])
        for i, (a, b) in enumerate((
            (wg_hbm, wg_s), (wu_hbm, wu_s), (wd_hbm, wd_s),
            (q_hbm, q_ref), (k_hbm, k_ref), (v_hbm, v_ref), (routes_hbm, routes_ref),
            (gates_hbm, gates_ref), (res_hbm, res_ref), (gain_hbm, gain_ref), (wo_hbm, w_all.at[h]),
        ))
    ]
    for i in (6, 7, 3, 4, 5, 8, 9, 10, 0, 1, 2):
        fetches[i].start()
    weights = fetches[:3]

    lane8 = iota((8, 128), 1)
    row8 = iota((8, 128), 0)

    scale = 1.0 / math.sqrt(128)
    tail = key_rows - min(tokens, key_rows)

    def level_lines(flat):
        hi = flat.astype(BF16).astype(F32)
        mid = (flat - hi).astype(BF16).astype(F32)
        lo = flat - hi - mid
        return jnp.where(
            row8 == 0, hi, jnp.where(row8 == 1, mid, jnp.where(row8 == 2, lo, 0.0))
        ).astype(BF16)

    def attend(j):
        q = q_ref[pl.ds(pl.multiple_of(j * 128, 128), 128), :]
        s = dot_nt(q, k_ref[...]) * scale
        token = j * 32 + parts(iota((128, key_rows - tail), 0), 4)[0]
        limit = (CTX * key_rows - tokens) - c * key_rows + token
        masked = jnp.where(
            tail + iota((128, key_rows - tail), 1) <= limit, s[:, tail:], jnp.float32(-1e30)
        )
        s = jnp.concatenate([s[:, :tail], masked], axis=1) if tail else masked
        m = jnp.max(s, axis=1, keepdims=True)
        w = jnp.exp(s - m)
        total = jnp.sum(w, axis=1, keepdims=True)
        o = (dot(w.astype(BF16), v_ref[...]) / total).astype(BF16)
        lse = m + jnp.log(total)
        flat = jnp.sum(
            jnp.where(iota((128, 128), 0) == iota((128, 128), 1), lse, 0.0), axis=0, keepdims=True
        )
        lines = level_lines(flat)
        for r in range(4):
            abuf[j * 4 + r, 0:32, :] = o[r * 32 : (r + 1) * 32, :]
            abuf[j * 4 + r, 32:40, :] = lines

    for i in (3, 4, 5):
        fetches[i].wait()

    other = at_z(1 - h)
    far_first = sorted(
        ((i, j) for i in range(X) for j in range(Y)),
        key=lambda d: -min(d[0], X - d[0]) - min(d[1], Y - d[1]),
    )

    def attend_side(hh):
        if Y % 4 == 0:
            side = rem(h + hh, 2) * (Y // 4)

            @pl.loop(0, PL // 4)
            def _(i):
                attend(div(i, Y // 4) * (Y // 2) + side + rem(i, Y // 4))

        elif hh:

            @pl.loop(0, CTX // 4)
            def _(i):
                attend(i)

    def send_side(hh):
        for i, j in far_first:
            if i or j:
                there = rem(x + i, X) * (2 * Y) + rem(y + j, Y)
                block = there + rem(h + hh, 2) * Y
                send(abuf.at[block], arecv.at[hh, p], ssem.at[0], a_sem.at[hh], there + h * Y, e)

    attend_side(1)
    fetches[10].wait()
    pl.semaphore_wait(barrier, CTX - 1 + 2 * (E - 1))
    send_side(1)

    send(w_all.at[h], w_all.at[h], ssem.at[7], early.at[0], other, e)

    attend_side(0)
    send_side(0)
    arecv[1, pl.ds(p, 1)] = abuf[pl.ds(other, 1)]
    arecv[0, pl.ds(p, 1)] = abuf[pl.ds(c, 1)]
    fetches[8].wait()
    fetches[9].wait()

    new, old = iota((32, 32), 0), iota((32, 32), 1)
    head, token = parts(new, 8)
    swap_s[...] = jnp.where(old == token * 4 + head, 1.0, 0.0).astype(BF16)
    high, s4 = parts(iota((S, S), 0), CAP)
    plane, zz = parts(high, 2)
    order_s[...] = jnp.where(
        iota((S, S), 1) == zz * (PL * CAP) + plane * CAP + s4, 1.0, 0.0
    ).astype(BF16)
    pick_rows = E * PB * CAP
    high, s4 = parts(iota((pick_rows, 128), 0), CAP)
    picks_s[...] = jnp.where(
        iota((pick_rows, 128), 1) == parts(high, PB)[0] * CAP + s4, 1.0, 0.0
    ).astype(BF16)
    high, _ = parts(iota((pick_rows, PB * 8), 0), CAP)
    mask_s[...] = jnp.where(
        parts(high, PB)[1] == parts(iota((pick_rows, PB * 8), 1), 8)[0], 1.0, 0.0
    )
    fetches[6].wait()
    fetches[7].wait()

    diagonal = iota((8, 8), 0) == iota((8, 8), 1)
    route = [
        jnp.sum(
            jnp.where(diagonal, routes_ref[k : k + 1, :].astype(F32), 0.0), axis=1, keepdims=True
        ).astype(jnp.int32)
        for k in range(2)
    ]
    gate = [
        jnp.sum(jnp.where(diagonal, gates_ref[k : k + 1, :], 0.0), axis=1, keepdims=True)
        for k in range(2)
    ]
    hit = jnp.where((lane8 == route[0]) | (lane8 == route[1]), 1.0, 0.0)
    before = jnp.zeros((8, 128), F32)
    for t in range(7):
        before = before + jnp.where(row8 > t, hit[t : t + 1, :], 0.0)
    slot = [
        jnp.sum(jnp.where(lane8 == route[k], before, 0.0), axis=1, keepdims=True).astype(jnp.int32)
        for k in range(2)
    ]
    place = [route[k] * CAP + slot[k] for k in range(2)]
    g_own[...] = jnp.where((lane8 == place[0]) | (lane8 == place[1]), 1.0, 0.0)
    own_gates = jnp.where(lane8 == place[0], gate[0], 0.0) + jnp.where(
        lane8 == place[1], gate[1], 0.0
    )
    gg_all[pl.ds(h, 1)] = own_gates[None]
    row_s = iota((8, S), 1)
    high, s4 = parts(row_s, CAP)
    f_sel[...] = jnp.where(
        (high == h * PL + p) & (route[0] == e) & (slot[0] == s4), 1.0, 0.0
    ).astype(BF16)

    send(gg_all.at[h], gg_all.at[h], ssem.at[8], early.at[1], at_z(1 - h), e)
    spread = div(p, PB) == e
    mine = rem(p, PB)

    @pl.when(spread)
    def _():
        @pl.loop(1, PL)
        def _(i):
            pp = rem(p + i, PL)
            there = at_plane(pp)
            low = div(pp, Y) * (2 * Y) + rem(pp, Y)
            for half in range(2):
                cols = pl.ds(pl.multiple_of((low + half * Y) * 128, 128), 128)
                send(res_ref.at[:, cols], res_recv.at[mine, half], ssem.at[9], early.at[2 + mine], there, e)
            send(g_own, g_recv.at[mine], ssem.at[10], early.at[2 + PB + mine], there, e)

        low = x * (2 * Y) + y
        for half in range(2):
            cols = pl.ds(pl.multiple_of((low + half * Y) * 128, 128), 128)
            res_recv[pl.ds(mine, 1), half] = res_ref[:, cols][None]
        g_recv[pl.ds(mine, 1)] = g_own[...][None]

    def combine(pairs, block):
        levels = jnp.full((32, 128), -1e30, F32)
        for i, (_, lines) in enumerate(pairs):
            line = jnp.sum(lines(), axis=0, keepdims=True)
            levels = jnp.where(iota((32, 128), 0) == i, line, levels)
        top = jnp.max(levels, axis=0, keepdims=True)
        weight = jnp.exp(levels - top)
        total = jnp.sum(weight, axis=0, keepdims=True)
        weight = jnp.concatenate([weight / total, jnp.zeros((96, 128), F32)], axis=0)
        wt_s[...] = weight.T
        columns = wt_s[pl.ds(pl.multiple_of(rem(block, 4) * 32, 32), 32), :]
        attended = jnp.zeros((32, 128), F32)
        for i, (rows, _) in enumerate(pairs):
            attended = attended + rows() * columns[:, i : i + 1]
        return attended, top + jnp.log(total)

    def slab(ref, *at):
        return (
            lambda: ref[(*at, slice(0, 32))].astype(F32),
            lambda: ref[(*at, slice(32, 40))].astype(F32),
        )

    wait_bytes(arecv.at[1, pl.ds(0, PL - 1)], a_sem.at[1])
    attended, level = combine([slab(arecv, 1, i) for i in range(PL)], other)
    a_out[0:32, :] = attended.astype(BF16)
    a_out[32:40, :] = level_lines(level)
    send(a_out, a_in, ssem.at[14], early.at[2 + 2 * PB], other, e)

    wait_bytes(arecv.at[0, pl.ds(0, PL - 1)], a_sem.at[0])
    own_part, own_level = combine([slab(arecv, 0, i) for i in range(PL)], c)
    own_lines = jnp.where(row8 == 0, own_level, 0.0)
    wait_bytes(a_in, early.at[2 + 2 * PB])
    attended, _ = combine([(lambda: own_part, lambda: own_lines), slab(a_in)], c)
    heads = dot(swap_s[...], attended.astype(BF16)).reshape(4, 1, 8, 128)
    att_all[:, pl.ds(p, 1)] = heads.astype(BF16)
    for i, j in far_first:
        if i or j:
            there = rem(x + i, X) * (2 * Y) + h * Y + rem(y + j, Y)
            send(att_all.at[:, p], att_all.at[:, p], ssem.at[1], rsem.at[1], there, e)

    wait_bytes(w_all.at[h], early.at[0])
    wait_bytes(att_all.at[:, pl.ds(0, PL - 1)], rsem.at[1])
    rows = jnp.concatenate(
        [att_all[r].astype(F32).reshape(PL * 8, 128) for r in range(4)], axis=1
    ).astype(BF16)
    partial = dot(rows, jnp.concatenate([w_all[0], w_all[1]], axis=1))
    rs_send[...] = partial.reshape(E, PB * 8, 256).astype(BF16)
    rs_recv[pl.ds(e, 1)] = rs_send[pl.ds(e, 1)]

    for i in sorted(range(1, E), key=lambda i: abs(i - E // 2)):
        ee = rem(e + i, E)
        send(rs_send.at[ee], rs_recv.at[e], ssem.at[2], rsem.at[2], c, ee)

    for i in range(PB):

        @pl.when(p != e * PB + i)
        def _():
            wait_bytes(res_recv.at[i], early.at[2 + i])
            wait_bytes(g_recv.at[i], early.at[2 + PB + i])

    table = g_recv[...].reshape(PB * 8, 128).astype(BF16)
    picks = (dot_nt(picks_s[...], table) * mask_s[...]).astype(BF16)
    residual = jnp.concatenate(
        [
            jnp.concatenate([res_recv[i, half].astype(F32) for half in range(2)], axis=1)
            for i in range(PB)
        ],
        axis=0,
    )

    wait_bytes(rs_recv.at[pl.ds(0, E - 1)], rsem.at[2])
    stream = residual
    for i in range(E):
        stream = stream + rs_recv[i].astype(F32)
    z_send[...] = dot(picks, stream.astype(BF16)).reshape(E, PB * CAP, 256).astype(BF16)
    xall[pl.ds(p, 1), pl.ds(hz, 1)] = z_send[pl.ds(e, 1)][None]

    for i in sorted(range(1, 2 * E), key=lambda i: abs(i - E)):
        zz = rem(hz + i, 2 * E)
        ee = rem(zz, E)
        hh = div(zz, E)
        send(z_send.at[ee], xall.at[p, hz], ssem.at[3], z_sem.at[rem(hh + h, 2)], at_z(hh), ee)

    sq_acc[...] = jnp.zeros_like(sq_acc)
    accg[...] = jnp.zeros_like(accg)
    accu[...] = jnp.zeros_like(accu)
    weights[0].wait()
    weights[1].wait()

    def ctx_of(i, j):
        return rem(x + i, X) * (2 * Y) + h * Y + rem(y + j, Y)

    def source(i, j):
        return rem(x + X - i, X), rem(y + Y - j, Y)

    early_half = pl.ds(pl.multiple_of(h * E, E), E)
    late_half = pl.ds(pl.multiple_of((1 - h) * E, E), E)

    def expert_products(xx, yy):
        src = xx * Y + yy
        part = xall[src].astype(F32).reshape(S, 256)
        sq_acc[...] += part[:, :128] * part[:, :128] + part[:, 128:] * part[:, 128:]
        low = pl.multiple_of((xx * (2 * Y) + yy) * 128, 128)
        high = pl.multiple_of((xx * (2 * Y) + Y + yy) * 128, 128)
        gain = [gain_ref[pl.ds(xx * (2 * Y) + half * Y + yy, 1), :] for half in range(2)]
        scaled = (part * jnp.concatenate(gain, axis=1)).astype(BF16)
        for acc, w in ((accg, wg_s), (accu, wu_s)):
            block = jnp.concatenate([w[:, pl.ds(low, 128)], w[:, pl.ds(high, 128)]], axis=1)
            acc[...] += dot_nt(scaled, block)
        own = dot(f_sel[...], part.astype(BF16))
        sown[:, pl.ds(low, 128)] = own[:, :128]
        sown[:, pl.ds(high, 128)] = own[:, 128:]

    rows = sorted(((i, 0) for i in range(1, X)), key=lambda d: min(d[0], X - d[0]))
    columns = sorted(((0, j) for j in range(1, Y)), key=lambda d: min(d[1], Y - d[1]))

    def spread_half(half, first_sem):
        for i, j in rows + columns:
            block = xall.at[p, half]
            send(block, block, ssem.at[4], d_recv.at[first_sem + i * Y + j], ctx_of(i, j), e)

    def forward(i, j):
        xx, yy = source(i, j)
        half, first_sem = (early_half, 0) if i else (late_half, PL)
        block = xall.at[xx * Y + yy, half]
        wait_bytes(block, d_recv.at[first_sem + i * Y + j])
        for n in near_first(Y) if i else near_first(X):
            to = (0, n) if i else (n, 0)
            first = i * Y + n if i else n * Y + j
            send(block, block, ssem.at[4], d_recv.at[first_sem + first], ctx_of(*to), e)

    def direct_products(i, j):
        xx, yy = source(i, j)
        half, first_sem = (late_half, PL) if i else (early_half, 0)
        wait_bytes(xall.at[xx * Y + yy, half], d_recv.at[first_sem + i * Y + j])
        expert_products(xx, yy)

    wait_bytes(xall.at[p, pl.ds(0, E - 1)], z_sem.at[0])
    spread_half(early_half, 0)
    wait_bytes(xall.at[p, pl.ds(0, E)], z_sem.at[1])
    spread_half(late_half, PL)
    expert_products(x, y)
    for d in rows + columns[:2]:
        forward(*d)
    for d in rows[:2]:
        direct_products(*d)
    for d in columns[2:]:
        forward(*d)
    for d in rows[2:] + columns:
        direct_products(*d)

    @pl.loop(0, (X - 1) * (Y - 1))
    def _(t):
        i, j = div(t, Y - 1) + 1, rem(t, Y - 1) + 1
        xx, yy = source(i, j)
        src = xx * Y + yy
        wait_bytes(xall.at[src, early_half], d_recv.at[i * Y + j])
        wait_bytes(xall.at[src, late_half], d_recv.at[PL + i * Y + j])
        expert_products(xx, yy)

    norm = lax.rsqrt(jnp.sum(sq_acc[...], axis=1, keepdims=True) / D + 1e-05)
    gate_val = accg[...] * norm
    act = ((gate_val / (1.0 + jnp.exp(-gate_val))) * (accu[...] * norm)).astype(BF16)
    act = dot(order_s[...], act).astype(BF16)

    weights[2].wait()
    for n in range(NCH):
        down = dot(act, wd_s[:, n * chunk_cols : (n + 1) * chunk_cols])
        e_send[n] = down.reshape(X, Y, 2 * CAP, chunk_cols).astype(BF16)
        if n % 2 == 0:
            for j in near_first(Y):
                block = e_send.at[n, :, rem(y + j, Y)]
                send(block, e_recv.at[n, j - 1, pl.ds(0, X)], ssem.at[5], e_sem.at[n], ctx_of(0, j), e)
        else:
            for i in near_first(X):
                block = e_send.at[n, rem(x + i, X)]
                send(block, e_recv.at[n, i - 1, pl.ds(0, Y)], ssem.at[11], e_sem.at[n], ctx_of(i, 0), e)

    for n in range(NCH):
        if n % 2 == 0:
            wait_bytes(e_recv.at[n, pl.ds(0, Y - 1), pl.ds(0, X)], e_sem.at[n])
            line = e_send[n, :, pl.ds(y, 1)].reshape(X, 2 * CAP, chunk_cols).astype(F32)
            for j in range(Y - 1):
                line = line + e_recv[n, j, :X].astype(F32)
            t_send[n, :X] = line.astype(BF16)
            for i in near_first(X):
                block = t_send.at[n, rem(x + i, X)]
                send(block, t_recv.at[n, i - 1], ssem.at[12], t_sem.at[n], ctx_of(i, 0), e)
        else:
            wait_bytes(e_recv.at[n, pl.ds(0, X - 1), pl.ds(0, Y)], e_sem.at[n])
            line = e_send[n, pl.ds(x, 1)].reshape(Y, 2 * CAP, chunk_cols).astype(F32)
            for i in range(X - 1):
                line = line + e_recv[n, i, :Y].astype(F32)
            t_send[n, :Y] = line.astype(BF16)
            for j in near_first(Y):
                block = t_send.at[n, rem(y + j, Y)]
                send(block, t_recv.at[n, j - 1], ssem.at[13], t_sem.at[n], ctx_of(0, j), e)

    wait_bytes(gg_all.at[h], early.at[1])
    weigh = [
        [
            jnp.sum(jnp.where(lane8 == e * CAP + s, gg_all[hh], 0.0), axis=1, keepdims=True)
            for s in range(CAP)
        ]
        for hh in range(2)
    ]
    for n in range(NCH):
        peers, mine = (X - 1, x) if n % 2 == 0 else (Y - 1, y)
        wait_bytes(t_recv.at[n, pl.ds(0, peers)], t_sem.at[n])
        total = t_send[n, mine].astype(F32)
        for i in range(peers):
            total = total + t_recv[n, i].astype(F32)
        for f in range(chunk_cols // CE):
            ee = n * (chunk_cols // CE) + f
            stream_own = sown[:, ee * CE : (ee + 1) * CE]
            for hh in range(2):
                term = jnp.where(h == hh, stream_own, 0.0)
                for s in range(CAP):
                    line = hh * CAP + s
                    term = term + weigh[hh][s] * total[line : line + 1, f * CE : (f + 1) * CE]
                f_send[hh * E + ee] = term.astype(BF16)
                away = (h != hh) | (e != ee)

                @pl.when(away)
                def _():
                    send(f_send.at[hh * E + ee], f_recv.at[hz], ssem.at[6], rsem.at[4], at_z(hh), ee)

    f_recv[pl.ds(hz, 1)] = f_send[pl.ds(hz, 1)]
    wait_bytes(f_recv.at[pl.ds(0, 2 * E - 1)], rsem.at[4])
    out_s[...] = jnp.sum(f_recv[...].astype(F32), axis=0).astype(BF16)
    result = pltpu.make_async_copy(out_s, out_hbm, wsem.at[0])
    result.start()

    wait_bytes(abuf.at[pl.ds(0, 2 * (PL - 1))], ssem.at[0])
    wait_bytes(a_out, ssem.at[14])
    wait_bytes(att_all.at[:, pl.ds(0, PL - 1)], ssem.at[1])
    wait_bytes(rs_send.at[pl.ds(0, E - 1)], ssem.at[2])
    wait_bytes(xall.at[0, pl.ds(0, 2 * E - 1)], ssem.at[3])
    wait_bytes(xall.at[pl.ds(0, PL - 1)], ssem.at[4])
    even, odd = pl.ds(0, (NCH + 1) // 2), pl.ds(0, NCH // 2)
    wait_bytes(e_send.at[even, :, pl.ds(0, Y - 1)], ssem.at[5])
    wait_bytes(e_send.at[odd, pl.ds(0, X - 1)], ssem.at[11])
    wait_bytes(t_send.at[even, pl.ds(0, X - 1)], ssem.at[12])
    wait_bytes(t_send.at[odd, pl.ds(0, Y - 1)], ssem.at[13])
    wait_bytes(f_send.at[pl.ds(0, 2 * E - 1)], ssem.at[6])
    wait_bytes(w_all.at[h], ssem.at[7])
    wait_bytes(gg_all.at[h], ssem.at[8])

    @pl.when(spread)
    def _():
        wait_bytes(f_recv.at[pl.ds(0, PL - 1), :, pl.ds(0, 256)], ssem.at[9])
        wait_bytes(f_recv.at[pl.ds(0, PL - 1), :, pl.ds(0, 256)], ssem.at[10])
    result.wait()


def local(queries, keys, values, out_proj, residual, gain, routes, gates, w_gate, w_up, w_down):
    X, Y = PLANE
    CTX, PL, E = 2 * X * Y, X * Y, lax.axis_size("exp")
    PB, D, FF = PL // E, gain.shape[0], w_gate.shape[2]
    S, CE = 2 * PL * CAP, D // E
    chunk_cols, side = 512, max(X, Y)
    NCH = D // chunk_cols
    return pl.pallas_call(
        functools.partial(kernel, (X, Y, E, chunk_cols)),
        out_shape=jax.ShapeDtypeStruct((8, CE), BF16),
        in_specs=[pl.BlockSpec(memory_space=pl.ANY)] * 11,
        out_specs=pl.BlockSpec(memory_space=pl.ANY),
        scratch_shapes=[
            pltpu.VMEM((8, CE), BF16),
            pltpu.VMEM((CTX * 32, 128), BF16),
            pltpu.VMEM((keys.shape[0], 128), BF16),
            pltpu.VMEM((keys.shape[0], 128), BF16),
            pltpu.VMEM((8, D), BF16),
            pltpu.VMEM((CTX, 128), F32),
            pltpu.VMEM((2, 8), jnp.int32),
            pltpu.VMEM((2, 8), F32),
            pltpu.VMEM((32, 32), BF16),
            pltpu.VMEM((S, S), BF16),
            pltpu.VMEM((E * PB * CAP, 128), BF16),
            pltpu.VMEM((E * PB * CAP, PB * 8), F32),
            pltpu.VMEM((CTX, 40, 128), BF16),
            pltpu.VMEM((2, PL, 40, 128), BF16),
            pltpu.VMEM((40, 128), BF16),
            pltpu.VMEM((40, 128), BF16),
            pltpu.VMEM((128, 128), F32),
            pltpu.VMEM((4, PL, 8, 128), BF16),
            pltpu.VMEM((2, 512, 128), BF16),
            pltpu.VMEM((E, PB * 8, 256), BF16),
            pltpu.VMEM((E, PB * 8, 256), BF16),
            pltpu.VMEM((PB, 2, 8, 128), BF16),
            pltpu.VMEM((8, 128), F32),
            pltpu.VMEM((PB, 8, 128), F32),
            pltpu.VMEM((2, 8, 128), F32),
            pltpu.VMEM((8, S), BF16),
            pltpu.VMEM((E, PB * CAP, 256), BF16),
            pltpu.VMEM((PL, 2 * E, PB * CAP, 256), BF16),
            pltpu.VMEM((S, 128), F32),
            pltpu.VMEM((S, FF), F32),
            pltpu.VMEM((S, FF), F32),
            pltpu.VMEM((8, D), F32),
            pltpu.VMEM((NCH, X, Y, 2 * CAP, chunk_cols), BF16),
            pltpu.VMEM((NCH, side - 1, side, 2 * CAP, chunk_cols), BF16),
            pltpu.VMEM((NCH, side, 2 * CAP, chunk_cols), BF16),
            pltpu.VMEM((NCH, side - 1, 2 * CAP, chunk_cols), BF16),
            pltpu.VMEM((2 * E, 8, CE), BF16),
            pltpu.VMEM((2 * E, 8, CE), BF16),
            pltpu.VMEM((FF, D), BF16),
            pltpu.VMEM((FF, D), BF16),
            pltpu.VMEM((FF, D), BF16),
            pltpu.SemaphoreType.DMA((11,)),
            pltpu.SemaphoreType.DMA((15,)),
            pltpu.SemaphoreType.DMA((2,)),
            pltpu.SemaphoreType.DMA((2,)),
            pltpu.SemaphoreType.DMA((5,)),
            pltpu.SemaphoreType.DMA((3 + 2 * PB,)),
            pltpu.SemaphoreType.DMA((2 * PL,)),
            pltpu.SemaphoreType.DMA((NCH,)),
            pltpu.SemaphoreType.DMA((NCH,)),
        ],
        compiler_params=pltpu.CompilerParams(
            collective_id=0, has_side_effects=True, vmem_limit_bytes=VMEM_LIMIT
        ),
    )(
        queries.reshape(CTX * 32, 128),
        keys.reshape(keys.shape[0], 128),
        values.reshape(values.shape[0], 128),
        out_proj,
        residual,
        gain.reshape(CTX, 128),
        routes.T,
        gates.T,
        jnp.swapaxes(w_gate, 1, 2).reshape(FF, D),
        jnp.swapaxes(w_up, 1, 2).reshape(FF, D),
        w_down.reshape(FF, D),
    )


def solution(mesh):
    return jax.shard_map(
        local,
        mesh=mesh,
        in_specs=(
            P(None, "exp", None),
            P("ctx", "exp", None),
            P("ctx", "exp", None),
            P("exp", "ctx"),
            P("ctx", None),
            P(),
            P("ctx", None),
            P("ctx", None),
            P("exp", None, "ctx"),
            P("exp", None, "ctx"),
            P("exp", "ctx", None),
        ),
        out_specs=P("ctx", "exp"),
        check_vma=False,
    )
```

```python
import functools
import math

import jax
import jax.numpy as jnp
from jax import lax
from jax.experimental import pallas as pl
from jax.experimental.pallas import tpu as pltpu
from jax.sharding import PartitionSpec as P

F32 = jnp.float32
BF16 = jnp.bfloat16
PLANE = (4, 4)
CAP = 4
VMEM_LIMIT = 56 * 1024 * 1024


def iota(shape, dim):
    return lax.broadcasted_iota(jnp.int32, shape, dim)


def div(a, b):
    return lax.div(a, jnp.int32(b))


def rem(a, b):
    return lax.rem(a, jnp.int32(b))


def parts(a, n):
    assert n & (n - 1) == 0
    return lax.shift_right_logical(a, jnp.int32(n.bit_length() - 1)), a & (n - 1)


def dot(a, b):
    return lax.dot_general(a, b, (((1,), (0,)), ((), ())), preferred_element_type=F32)


def dot_nt(a, b):
    return lax.dot_general(a, b, (((1,), (1,)), ((), ())), preferred_element_type=F32)


def near_first(n):
    return sorted(range(1, n), key=lambda i: min(i, n - i))


def far_peers(n):
    return near_first(n)[::-1]


def wait_bytes(ref, sem):
    pltpu.make_async_copy(ref, ref, sem).wait()


def kernel(
    geom,
    q_hbm, k_hbm, v_hbm, wo_hbm, res_hbm, gain_hbm, routes_hbm, gates_hbm, wg_hbm, wu_hbm, wd_hbm,
    out_hbm,
    out_s, q_ref, k_ref, v_ref, res_ref, gain_ref, routes_ref, gates_ref, swap_s, order_s, picks_s, mask_s,
    abuf, arecv, a_out, a_in, wt_s, att_all, w_all, rs_send, rs_recv, res_recv, g_own, g_recv, gg_all, f_sel,
    z_send, xall, sq_acc, accg, accu, sown, e_send, e_recv, t_send, t_recv, f_send, f_recv,
    wg_s, wu_s, wd_s,
    wsem, ssem, a_sem, z_sem, rsem, early, d_recv, e_sem, t_sem,
):
    X, Y, E, chunk_cols = geom
    PL, CTX = X * Y, 2 * X * Y
    PB = PL // E
    D = CTX * 128
    S = 2 * PL * CAP
    NCH, CE = D // chunk_cols, D // E
    tokens = CTX * 8
    key_rows = k_ref.shape[0]

    c = lax.axis_index("ctx")
    e = lax.axis_index("exp")
    x = div(c, 2 * Y)
    h = rem(div(c, Y), 2)
    y = rem(c, Y)
    p = x * Y + y
    hz = h * E + e

    def at_plane(pp):
        return div(pp, Y) * (2 * Y) + h * Y + rem(pp, Y)

    def at_z(hh):
        return x * (2 * Y) + hh * Y + y

    def send(src, dst, ssem_, rsem_, ctx, exp):
        pltpu.make_async_remote_copy(
            src_ref=src, dst_ref=dst, send_sem=ssem_, recv_sem=rsem_,
            device_id={"ctx": ctx, "exp": exp}, device_id_type=pl.DeviceIdType.MESH,
        ).start()

    barrier = pltpu.get_barrier_semaphore()

    for i in range(X):
        for hh in range(2):
            for j in range(Y):
                there = rem(x + i, X) * (2 * Y) + rem(h + hh, 2) * Y + rem(y + j, Y)
                if i or hh or j:
                    pl.semaphore_signal(
                        barrier, inc=1, device_id={"ctx": there, "exp": e},
                        device_id_type=pl.DeviceIdType.MESH,
                    )
    for i in range(1, E):
        for hh in range(2):
            pl.semaphore_signal(
                barrier, inc=1, device_id={"ctx": at_z(hh), "exp": rem(e + i, E)},
                device_id_type=pl.DeviceIdType.MESH,
            )

    fetches = [
        pltpu.make_async_copy(a, b, wsem.at[i])
        for i, (a, b) in enumerate((
            (wg_hbm, wg_s), (wu_hbm, wu_s), (wd_hbm, wd_s),
            (q_hbm, q_ref), (k_hbm, k_ref), (v_hbm, v_ref), (routes_hbm, routes_ref),
            (gates_hbm, gates_ref), (res_hbm, res_ref), (gain_hbm, gain_ref), (wo_hbm, w_all.at[h]),
        ))
    ]
    for i in (6, 7, 3, 4, 5, 8, 9, 10, 0, 1, 2):
        fetches[i].start()
    weights = fetches[:3]

    lane8 = iota((8, 128), 1)
    row8 = iota((8, 128), 0)

    scale = 1.0 / math.sqrt(128)
    tail = key_rows - min(tokens, key_rows)

    def level_lines(flat):
        hi = flat.astype(BF16).astype(F32)
        mid = (flat - hi).astype(BF16).astype(F32)
        lo = flat - hi - mid
        return jnp.where(
            row8 == 0, hi, jnp.where(row8 == 1, mid, jnp.where(row8 == 2, lo, 0.0))
        ).astype(BF16)

    def attend(j):
        q = q_ref[pl.ds(pl.multiple_of(j * 128, 128), 128), :]
        s = dot_nt(q, k_ref[...]) * scale
        token = j * 32 + parts(iota((128, key_rows - tail), 0), 4)[0]
        limit = (CTX * key_rows - tokens) - c * key_rows + token
        masked = jnp.where(
            tail + iota((128, key_rows - tail), 1) <= limit, s[:, tail:], jnp.float32(-1e30)
        )
        s = jnp.concatenate([s[:, :tail], masked], axis=1) if tail else masked
        m = jnp.max(s, axis=1, keepdims=True)
        w = jnp.exp(s - m)
        total = jnp.sum(w, axis=1, keepdims=True)
        o = (dot(w.astype(BF16), v_ref[...]) / total).astype(BF16)
        lse = m + jnp.log(total)
        flat = jnp.sum(
            jnp.where(iota((128, 128), 0) == iota((128, 128), 1), lse, 0.0), axis=0, keepdims=True
        )
        lines = level_lines(flat)
        for r in range(4):
            abuf[j * 4 + r, 0:32, :] = o[r * 32 : (r + 1) * 32, :]
            abuf[j * 4 + r, 32:40, :] = lines

    for i in (3, 4, 5):
        fetches[i].wait()

    other = at_z(1 - h)
    far_first = sorted(
        ((i, j) for i in range(X) for j in range(Y)),
        key=lambda d: -min(d[0], X - d[0]) - min(d[1], Y - d[1]),
    )

    def attend_side(hh):
        if Y % 4 == 0:
            side = rem(h + hh, 2) * (Y // 4)

            @pl.loop(0, PL // 4)
            def _(i):
                attend(div(i, Y // 4) * (Y // 2) + side + rem(i, Y // 4))

        elif hh:

            @pl.loop(0, CTX // 4)
            def _(i):
                attend(i)

    def send_side(hh):
        for i, j in far_first:
            if i or j:
                there = rem(x + i, X) * (2 * Y) + rem(y + j, Y)
                block = there + rem(h + hh, 2) * Y
                send(abuf.at[block], arecv.at[hh, p], ssem.at[0], a_sem.at[hh], there + h * Y, e)

    attend_side(1)
    fetches[10].wait()
    pl.semaphore_wait(barrier, CTX - 1 + 2 * (E - 1))
    send_side(1)

    send(w_all.at[h], w_all.at[h], ssem.at[7], early.at[0], other, e)

    attend_side(0)
    send_side(0)
    arecv[1, pl.ds(p, 1)] = abuf[pl.ds(other, 1)]
    arecv[0, pl.ds(p, 1)] = abuf[pl.ds(c, 1)]
    fetches[8].wait()
    fetches[9].wait()

    new, old = iota((32, 32), 0), iota((32, 32), 1)
    head, token = parts(new, 8)
    swap_s[...] = jnp.where(old == token * 4 + head, 1.0, 0.0).astype(BF16)
    high, s4 = parts(iota((S, S), 0), CAP)
    plane, zz = parts(high, 2)
    order_s[...] = jnp.where(
        iota((S, S), 1) == zz * (PL * CAP) + plane * CAP + s4, 1.0, 0.0
    ).astype(BF16)
    pick_rows = E * PB * CAP
    high, s4 = parts(iota((pick_rows, 128), 0), CAP)
    picks_s[...] = jnp.where(
        iota((pick_rows, 128), 1) == parts(high, PB)[0] * CAP + s4, 1.0, 0.0
    ).astype(BF16)
    high, _ = parts(iota((pick_rows, PB * 8), 0), CAP)
    mask_s[...] = jnp.where(
        parts(high, PB)[1] == parts(iota((pick_rows, PB * 8), 1), 8)[0], 1.0, 0.0
    )
    fetches[6].wait()
    fetches[7].wait()

    diagonal = iota((8, 8), 0) == iota((8, 8), 1)
    route = [
        jnp.sum(
            jnp.where(diagonal, routes_ref[k : k + 1, :].astype(F32), 0.0), axis=1, keepdims=True
        ).astype(jnp.int32)
        for k in range(2)
    ]
    gate = [
        jnp.sum(jnp.where(diagonal, gates_ref[k : k + 1, :], 0.0), axis=1, keepdims=True)
        for k in range(2)
    ]
    hit = jnp.where((lane8 == route[0]) | (lane8 == route[1]), 1.0, 0.0)
    before = jnp.zeros((8, 128), F32)
    for t in range(7):
        before = before + jnp.where(row8 > t, hit[t : t + 1, :], 0.0)
    slot = [
        jnp.sum(jnp.where(lane8 == route[k], before, 0.0), axis=1, keepdims=True).astype(jnp.int32)
        for k in range(2)
    ]
    place = [route[k] * CAP + slot[k] for k in range(2)]
    g_own[...] = jnp.where((lane8 == place[0]) | (lane8 == place[1]), 1.0, 0.0)
    own_gates = jnp.where(lane8 == place[0], gate[0], 0.0) + jnp.where(
        lane8 == place[1], gate[1], 0.0
    )
    gg_all[pl.ds(h, 1)] = own_gates[None]
    row_s = iota((8, S), 1)
    high, s4 = parts(row_s, CAP)
    f_sel[...] = jnp.where(
        (high == h * PL + p) & (route[0] == e) & (slot[0] == s4), 1.0, 0.0
    ).astype(BF16)

    send(gg_all.at[h], gg_all.at[h], ssem.at[8], early.at[1], at_z(1 - h), e)
    spread = div(p, PB) == e
    mine = rem(p, PB)

    @pl.when(spread)
    def _():
        @pl.loop(1, PL)
        def _(i):
            pp = rem(p + i, PL)
            there = at_plane(pp)
            low = div(pp, Y) * (2 * Y) + rem(pp, Y)
            for half in range(2):
                cols = pl.ds(pl.multiple_of((low + half * Y) * 128, 128), 128)
                send(res_ref.at[:, cols], res_recv.at[mine, half], ssem.at[9], early.at[2 + mine], there, e)
            send(g_own, g_recv.at[mine], ssem.at[10], early.at[2 + PB + mine], there, e)

        low = x * (2 * Y) + y
        for half in range(2):
            cols = pl.ds(pl.multiple_of((low + half * Y) * 128, 128), 128)
            res_recv[pl.ds(mine, 1), half] = res_ref[:, cols][None]
        g_recv[pl.ds(mine, 1)] = g_own[...][None]

    def combine(pairs, block):
        levels = jnp.full((32, 128), -1e30, F32)
        for i, (_, lines) in enumerate(pairs):
            line = jnp.sum(lines(), axis=0, keepdims=True)
            levels = jnp.where(iota((32, 128), 0) == i, line, levels)
        top = jnp.max(levels, axis=0, keepdims=True)
        weight = jnp.exp(levels - top)
        total = jnp.sum(weight, axis=0, keepdims=True)
        weight = jnp.concatenate([weight / total, jnp.zeros((96, 128), F32)], axis=0)
        wt_s[...] = weight.T
        columns = wt_s[pl.ds(pl.multiple_of(rem(block, 4) * 32, 32), 32), :]
        attended = jnp.zeros((32, 128), F32)
        for i, (rows, _) in enumerate(pairs):
            attended = attended + rows() * columns[:, i : i + 1]
        return attended, top + jnp.log(total)

    def slab(ref, *at):
        return (
            lambda: ref[(*at, slice(0, 32))].astype(F32),
            lambda: ref[(*at, slice(32, 40))].astype(F32),
        )

    wait_bytes(arecv.at[1, pl.ds(0, PL - 1)], a_sem.at[1])
    attended, level = combine([slab(arecv, 1, i) for i in range(PL)], other)
    a_out[0:32, :] = attended.astype(BF16)
    a_out[32:40, :] = level_lines(level)
    send(a_out, a_in, ssem.at[14], early.at[2 + 2 * PB], other, e)

    wait_bytes(arecv.at[0, pl.ds(0, PL - 1)], a_sem.at[0])
    own_part, own_level = combine([slab(arecv, 0, i) for i in range(PL)], c)
    own_lines = jnp.where(row8 == 0, own_level, 0.0)
    wait_bytes(a_in, early.at[2 + 2 * PB])
    attended, _ = combine([(lambda: own_part, lambda: own_lines), slab(a_in)], c)
    heads = dot(swap_s[...], attended.astype(BF16)).reshape(4, 1, 8, 128)
    att_all[:, pl.ds(p, 1)] = heads.astype(BF16)
    for i, j in far_first:
        if i or j:
            there = rem(x + i, X) * (2 * Y) + h * Y + rem(y + j, Y)
            send(att_all.at[:, p], att_all.at[:, p], ssem.at[1], rsem.at[1], there, e)

    wait_bytes(w_all.at[h], early.at[0])
    wait_bytes(att_all.at[:, pl.ds(0, PL - 1)], rsem.at[1])
    rows = jnp.concatenate(
        [att_all[r].astype(F32).reshape(PL * 8, 128) for r in range(4)], axis=1
    ).astype(BF16)
    partial = dot(rows, jnp.concatenate([w_all[0], w_all[1]], axis=1))
    rs_send[...] = partial.reshape(E, PB * 8, 256).astype(BF16)
    rs_recv[pl.ds(e, 1)] = rs_send[pl.ds(e, 1)]

    for i in sorted(range(1, E), key=lambda i: abs(i - E // 2)):
        ee = rem(e + i, E)
        send(rs_send.at[ee], rs_recv.at[e], ssem.at[2], rsem.at[2], c, ee)

    for i in range(PB):

        @pl.when(p != e * PB + i)
        def _():
            wait_bytes(res_recv.at[i], early.at[2 + i])
            wait_bytes(g_recv.at[i], early.at[2 + PB + i])

    table = g_recv[...].reshape(PB * 8, 128).astype(BF16)
    picks = (dot_nt(picks_s[...], table) * mask_s[...]).astype(BF16)
    residual = jnp.concatenate(
        [
            jnp.concatenate([res_recv[i, half].astype(F32) for half in range(2)], axis=1)
            for i in range(PB)
        ],
        axis=0,
    )

    wait_bytes(rs_recv.at[pl.ds(0, E - 1)], rsem.at[2])
    stream = residual
    for i in range(E):
        stream = stream + rs_recv[i].astype(F32)
    z_send[...] = dot(picks, stream.astype(BF16)).reshape(E, PB * CAP, 256).astype(BF16)
    xall[pl.ds(p, 1), pl.ds(hz, 1)] = z_send[pl.ds(e, 1)][None]

    for i in sorted(range(1, 2 * E), key=lambda i: abs(i - E)):
        zz = rem(hz + i, 2 * E)
        ee = rem(zz, E)
        hh = div(zz, E)
        send(z_send.at[ee], xall.at[p, hz], ssem.at[3], z_sem.at[rem(hh + h, 2)], at_z(hh), ee)

    sq_acc[...] = jnp.zeros_like(sq_acc)
    accg[...] = jnp.zeros_like(accg)
    accu[...] = jnp.zeros_like(accu)
    weights[0].wait()
    weights[1].wait()

    def ctx_of(i, j):
        return rem(x + i, X) * (2 * Y) + h * Y + rem(y + j, Y)

    def source(i, j):
        return rem(x + X - i, X), rem(y + Y - j, Y)

    early_half = pl.ds(pl.multiple_of(h * E, E), E)
    late_half = pl.ds(pl.multiple_of((1 - h) * E, E), E)

    def expert_products(xx, yy):
        src = xx * Y + yy
        part = xall[src].astype(F32).reshape(S, 256)
        sq_acc[...] += part[:, :128] * part[:, :128] + part[:, 128:] * part[:, 128:]
        low = pl.multiple_of((xx * (2 * Y) + yy) * 128, 128)
        high = pl.multiple_of((xx * (2 * Y) + Y + yy) * 128, 128)
        gain = [gain_ref[pl.ds(xx * (2 * Y) + half * Y + yy, 1), :] for half in range(2)]
        scaled = (part * jnp.concatenate(gain, axis=1)).astype(BF16)
        for acc, w in ((accg, wg_s), (accu, wu_s)):
            block = jnp.concatenate([w[:, pl.ds(low, 128)], w[:, pl.ds(high, 128)]], axis=1)
            acc[...] += dot_nt(scaled, block)
        own = dot(f_sel[...], part.astype(BF16))
        sown[:, pl.ds(low, 128)] = own[:, :128]
        sown[:, pl.ds(high, 128)] = own[:, 128:]

    rows = sorted(((i, 0) for i in range(1, X)), key=lambda d: min(d[0], X - d[0]))
    columns = sorted(((0, j) for j in range(1, Y)), key=lambda d: min(d[1], Y - d[1]))

    def spread_half(half, first_sem):
        for i, j in rows + columns:
            block = xall.at[p, half]
            send(block, block, ssem.at[4], d_recv.at[first_sem + i * Y + j], ctx_of(i, j), e)

    def forward(i, j):
        xx, yy = source(i, j)
        half, first_sem = (early_half, 0) if i else (late_half, PL)
        block = xall.at[xx * Y + yy, half]
        wait_bytes(block, d_recv.at[first_sem + i * Y + j])
        for n in near_first(Y) if i else near_first(X):
            to = (0, n) if i else (n, 0)
            first = i * Y + n if i else n * Y + j
            send(block, block, ssem.at[4], d_recv.at[first_sem + first], ctx_of(*to), e)

    def direct_products(i, j):
        xx, yy = source(i, j)
        half, first_sem = (late_half, PL) if i else (early_half, 0)
        wait_bytes(xall.at[xx * Y + yy, half], d_recv.at[first_sem + i * Y + j])
        expert_products(xx, yy)

    wait_bytes(xall.at[p, pl.ds(0, E - 1)], z_sem.at[0])
    spread_half(early_half, 0)
    wait_bytes(xall.at[p, pl.ds(0, E)], z_sem.at[1])
    spread_half(late_half, PL)
    expert_products(x, y)
    for d in rows + columns[:2]:
        forward(*d)
    for d in rows[:2]:
        direct_products(*d)
    for d in columns[2:]:
        forward(*d)
    for d in rows[2:] + columns:
        direct_products(*d)

    @pl.loop(0, (X - 1) * (Y - 1))
    def _(t):
        i, j = div(t, Y - 1) + 1, rem(t, Y - 1) + 1
        xx, yy = source(i, j)
        src = xx * Y + yy
        wait_bytes(xall.at[src, early_half], d_recv.at[i * Y + j])
        wait_bytes(xall.at[src, late_half], d_recv.at[PL + i * Y + j])
        expert_products(xx, yy)

    norm = lax.rsqrt(jnp.sum(sq_acc[...], axis=1, keepdims=True) / D + 1e-05)
    gate_val = accg[...] * norm
    act = ((gate_val / (1.0 + jnp.exp(-gate_val))) * (accu[...] * norm)).astype(BF16)
    act = dot(order_s[...], act).astype(BF16)

    weights[2].wait()
    for n in range(NCH):
        down = dot(act, wd_s[:, n * chunk_cols : (n + 1) * chunk_cols])
        e_send[n] = down.reshape(X, Y, 2 * CAP, chunk_cols).astype(BF16)
        if n % 2 == 0:
            for j in far_peers(Y):
                block = e_send.at[n, :, rem(y + j, Y)]
                send(block, e_recv.at[n, j - 1, pl.ds(0, X)], ssem.at[5], e_sem.at[n], ctx_of(0, j), e)
        else:
            for i in far_peers(X):
                block = e_send.at[n, rem(x + i, X)]
                send(block, e_recv.at[n, i - 1, pl.ds(0, Y)], ssem.at[11], e_sem.at[n], ctx_of(i, 0), e)

    for n in range(NCH):
        if n % 2 == 0:
            wait_bytes(e_recv.at[n, pl.ds(0, Y - 1), pl.ds(0, X)], e_sem.at[n])
            line = e_send[n, :, pl.ds(y, 1)].reshape(X, 2 * CAP, chunk_cols).astype(F32)
            for j in range(Y - 1):
                line = line + e_recv[n, j, :X].astype(F32)
            t_send[n, :X] = line.astype(BF16)
            for i in far_peers(X):
                block = t_send.at[n, rem(x + i, X)]
                send(block, t_recv.at[n, i - 1], ssem.at[12], t_sem.at[n], ctx_of(i, 0), e)
        else:
            wait_bytes(e_recv.at[n, pl.ds(0, X - 1), pl.ds(0, Y)], e_sem.at[n])
            line = e_send[n, pl.ds(x, 1)].reshape(Y, 2 * CAP, chunk_cols).astype(F32)
            for i in range(X - 1):
                line = line + e_recv[n, i, :Y].astype(F32)
            t_send[n, :Y] = line.astype(BF16)
            for j in far_peers(Y):
                block = t_send.at[n, rem(y + j, Y)]
                send(block, t_recv.at[n, j - 1], ssem.at[13], t_sem.at[n], ctx_of(0, j), e)

    wait_bytes(gg_all.at[h], early.at[1])
    weigh = [
        [
            jnp.sum(jnp.where(lane8 == e * CAP + s, gg_all[hh], 0.0), axis=1, keepdims=True)
            for s in range(CAP)
        ]
        for hh in range(2)
    ]
    for n in range(NCH):
        peers, mine = (X - 1, x) if n % 2 == 0 else (Y - 1, y)
        wait_bytes(t_recv.at[n, pl.ds(0, peers)], t_sem.at[n])
        total = t_send[n, mine].astype(F32)
        for i in range(peers):
            total = total + t_recv[n, i].astype(F32)
        for f in range(chunk_cols // CE):
            ee = n * (chunk_cols // CE) + f
            stream_own = sown[:, ee * CE : (ee + 1) * CE]
            for hh in range(2):
                term = jnp.where(h == hh, stream_own, 0.0)
                for s in range(CAP):
                    line = hh * CAP + s
                    term = term + weigh[hh][s] * total[line : line + 1, f * CE : (f + 1) * CE]
                f_send[hh * E + ee] = term.astype(BF16)
                away = (h != hh) | (e != ee)

                @pl.when(away)
                def _():
                    send(f_send.at[hh * E + ee], f_recv.at[hz], ssem.at[6], rsem.at[4], at_z(hh), ee)

    f_recv[pl.ds(hz, 1)] = f_send[pl.ds(hz, 1)]
    wait_bytes(f_recv.at[pl.ds(0, 2 * E - 1)], rsem.at[4])
    out_s[...] = jnp.sum(f_recv[...].astype(F32), axis=0).astype(BF16)
    result = pltpu.make_async_copy(out_s, out_hbm, wsem.at[0])
    result.start()

    wait_bytes(abuf.at[pl.ds(0, 2 * (PL - 1))], ssem.at[0])
    wait_bytes(a_out, ssem.at[14])
    wait_bytes(att_all.at[:, pl.ds(0, PL - 1)], ssem.at[1])
    wait_bytes(rs_send.at[pl.ds(0, E - 1)], ssem.at[2])
    wait_bytes(xall.at[0, pl.ds(0, 2 * E - 1)], ssem.at[3])
    wait_bytes(xall.at[pl.ds(0, PL - 1)], ssem.at[4])
    even, odd = pl.ds(0, (NCH + 1) // 2), pl.ds(0, NCH // 2)
    wait_bytes(e_send.at[even, :, pl.ds(0, Y - 1)], ssem.at[5])
    wait_bytes(e_send.at[odd, pl.ds(0, X - 1)], ssem.at[11])
    wait_bytes(t_send.at[even, pl.ds(0, X - 1)], ssem.at[12])
    wait_bytes(t_send.at[odd, pl.ds(0, Y - 1)], ssem.at[13])
    wait_bytes(f_send.at[pl.ds(0, 2 * E - 1)], ssem.at[6])
    wait_bytes(w_all.at[h], ssem.at[7])
    wait_bytes(gg_all.at[h], ssem.at[8])

    @pl.when(spread)
    def _():
        wait_bytes(f_recv.at[pl.ds(0, PL - 1), :, pl.ds(0, 256)], ssem.at[9])
        wait_bytes(f_recv.at[pl.ds(0, PL - 1), :, pl.ds(0, 256)], ssem.at[10])
    result.wait()


def local(queries, keys, values, out_proj, residual, gain, routes, gates, w_gate, w_up, w_down):
    X, Y = PLANE
    CTX, PL, E = 2 * X * Y, X * Y, lax.axis_size("exp")
    PB, D, FF = PL // E, gain.shape[0], w_gate.shape[2]
    S, CE = 2 * PL * CAP, D // E
    chunk_cols, side = 512, max(X, Y)
    NCH = D // chunk_cols
    return pl.pallas_call(
        functools.partial(kernel, (X, Y, E, chunk_cols)),
        out_shape=jax.ShapeDtypeStruct((8, CE), BF16),
        in_specs=[pl.BlockSpec(memory_space=pl.ANY)] * 11,
        out_specs=pl.BlockSpec(memory_space=pl.ANY),
        scratch_shapes=[
            pltpu.VMEM((8, CE), BF16),
            pltpu.VMEM((CTX * 32, 128), BF16),
            pltpu.VMEM((keys.shape[0], 128), BF16),
            pltpu.VMEM((keys.shape[0], 128), BF16),
            pltpu.VMEM((8, D), BF16),
            pltpu.VMEM((CTX, 128), F32),
            pltpu.VMEM((2, 8), jnp.int32),
            pltpu.VMEM((2, 8), F32),
            pltpu.VMEM((32, 32), BF16),
            pltpu.VMEM((S, S), BF16),
            pltpu.VMEM((E * PB * CAP, 128), BF16),
            pltpu.VMEM((E * PB * CAP, PB * 8), F32),
            pltpu.VMEM((CTX, 40, 128), BF16),
            pltpu.VMEM((2, PL, 40, 128), BF16),
            pltpu.VMEM((40, 128), BF16),
            pltpu.VMEM((40, 128), BF16),
            pltpu.VMEM((128, 128), F32),
            pltpu.VMEM((4, PL, 8, 128), BF16),
            pltpu.VMEM((2, 512, 128), BF16),
            pltpu.VMEM((E, PB * 8, 256), BF16),
            pltpu.VMEM((E, PB * 8, 256), BF16),
            pltpu.VMEM((PB, 2, 8, 128), BF16),
            pltpu.VMEM((8, 128), F32),
            pltpu.VMEM((PB, 8, 128), F32),
            pltpu.VMEM((2, 8, 128), F32),
            pltpu.VMEM((8, S), BF16),
            pltpu.VMEM((E, PB * CAP, 256), BF16),
            pltpu.VMEM((PL, 2 * E, PB * CAP, 256), BF16),
            pltpu.VMEM((S, 128), F32),
            pltpu.VMEM((S, FF), F32),
            pltpu.VMEM((S, FF), F32),
            pltpu.VMEM((8, D), F32),
            pltpu.VMEM((NCH, X, Y, 2 * CAP, chunk_cols), BF16),
            pltpu.VMEM((NCH, side - 1, side, 2 * CAP, chunk_cols), BF16),
            pltpu.VMEM((NCH, side, 2 * CAP, chunk_cols), BF16),
            pltpu.VMEM((NCH, side - 1, 2 * CAP, chunk_cols), BF16),
            pltpu.VMEM((2 * E, 8, CE), BF16),
            pltpu.VMEM((2 * E, 8, CE), BF16),
            pltpu.VMEM((FF, D), BF16),
            pltpu.VMEM((FF, D), BF16),
            pltpu.VMEM((FF, D), BF16),
            pltpu.SemaphoreType.DMA((11,)),
            pltpu.SemaphoreType.DMA((15,)),
            pltpu.SemaphoreType.DMA((2,)),
            pltpu.SemaphoreType.DMA((2,)),
            pltpu.SemaphoreType.DMA((5,)),
            pltpu.SemaphoreType.DMA((3 + 2 * PB,)),
            pltpu.SemaphoreType.DMA((2 * PL,)),
            pltpu.SemaphoreType.DMA((NCH,)),
            pltpu.SemaphoreType.DMA((NCH,)),
        ],
        compiler_params=pltpu.CompilerParams(
            collective_id=0, has_side_effects=True, vmem_limit_bytes=VMEM_LIMIT
        ),
    )(
        queries.reshape(CTX * 32, 128),
        keys.reshape(keys.shape[0], 128),
        values.reshape(values.shape[0], 128),
        out_proj,
        residual,
        gain.reshape(CTX, 128),
        routes.T,
        gates.T,
        jnp.swapaxes(w_gate, 1, 2).reshape(FF, D),
        jnp.swapaxes(w_up, 1, 2).reshape(FF, D),
        w_down.reshape(FF, D),
    )


def solution(mesh):
    return jax.shard_map(
        local,
        mesh=mesh,
        in_specs=(
            P(None, "exp", None),
            P("ctx", "exp", None),
            P("ctx", "exp", None),
            P("exp", "ctx"),
            P("ctx", None),
            P(),
            P("ctx", None),
            P("ctx", None),
            P("exp", None, "ctx"),
            P("exp", None, "ctx"),
            P("exp", "ctx", None),
        ),
        out_specs=P("ctx", "exp"),
        check_vma=False,
    )
```
